32 devices in a mesh: groups: 2 (over y), tensor: 16 (over z, x, core).
Axes of the slice: x: 2, y: 2, z: 4, core: 2. Of those that a mesh axis runs over, the one named last changes fastest.
Arguments:
- token_ids: int32 [16, 4], P('tensor', 'groups'), parts along dimension 1, may hold values from 0 to 63
- lengths: int32 [4], P('groups'), parts along dimension 0, may hold values from 8 to 16, as said below
- embed_table: bfloat16 [64, 6144], replicated, may hold values from -6 to 6
- gain_attn: float32 [6144], replicated, may hold values from 0.1 to 1.9
- w_qkv: bfloat16 [6144, 18432], P(None, 'tensor'), may hold values from -0.078125 to 0.078125
- w_out: bfloat16 [6144, 6144], P(None, 'tensor'), may hold values from -0.078125 to 0.078125
- gain_first: float32 [6144], replicated, may hold values from 0.1 to 1.9
- gate_first: bfloat16 [6144, 16384], P(None, 'tensor'), may hold values from -0.078125 to 0.078125
- up_first: bfloat16 [6144, 16384], P(None, 'tensor'), may hold values from -0.078125 to 0.078125
- down_first: bfloat16 [16384, 6144], P('tensor'), may hold values from -0.09375 to 0.09375
- gain_second: float32 [6144], replicated, may hold values from 0.1 to 1.9
- gate_second: bfloat16 [6144, 16384], P(None, 'tensor'), may hold values from -0.078125 to 0.078125
- up_second: bfloat16 [6144, 16384], P(None, 'tensor'), may hold values from -0.078125 to 0.078125
- down_second: bfloat16 [16384, 6144], P('tensor'), may hold values from -0.09375 to 0.09375
Outputs:
- states: bfloat16 [16, 4, 6144], P('tensor', 'groups'), parts along dimension 1
The draws below stay inside these ranges and needn't reach their ends.
There are 2 independent parts, one for each index of `groups`. The reference program is written for one: setup_inputs(seed, part) draws one part's arguments, and reference() takes and returns one part's arrays. A program takes and returns all parts, laid end to end along the dimension named above; an argument that names none is the same for every part. Nothing has to cross between parts.
Inputs may be any that keep to these rules, and one draw needn't show every extreme that they name: `lengths`: each micro-batch holds one protein of at least half of 16 positions; in every draw one micro-batch is full, 16 positions.
All inputs are finite; a program needn't handle non-finite values.
Results may differ from the reference program's by a relative error of at most 0.013.
Values may be sent and summed in bfloat16 or wider, within the bound.
No kernel may reach another device: no remote copies, remote signals or barrier semaphores. Data moves between devices by JAX's collectives and lax.ppermute only.
A program may use at most 192 MiB of HBM per device.

```python
import jax
import jax.numpy as jnp
from jax import lax

D = 6144
H = 48
HD = 128
VOCAB = 64
FFW = 16384
MICRO = 2
MB_TOK = 16


def draw_lengths(key, part):
    first_key, second_key = jax.random.split(jax.random.fold_in(key, 17))
    base_len = jax.random.randint(first_key, (MICRO,), MB_TOK // 2, MB_TOK + 1)
    full_index = jax.random.randint(second_key, (), 0, MICRO)
    return jnp.where(jnp.arange(MICRO) == full_index, MB_TOK, base_len).astype(jnp.int32)


def place_ends(result, rng, least, top_value):
    index_at = [jax.random.randint(jax.random.fold_in(rng, axis), (), 0, length) for axis, length in enumerate(result.shape)]
    widest = result.shape.index(max(result.shape))
    beside = index_at[:widest] + [(index_at[widest] + 1) % result.shape[widest]] + index_at[widest + 1:]
    return result.at[tuple(index_at)].set(least).at[tuple(beside)].set(top_value)


def block_scale(rng, extent, cuts, low, high):
    factor_of = 1.0
    for axis_at, shards_of in cuts:
        heights = jax.random.uniform(jax.random.fold_in(jax.random.fold_in(rng, 6), axis_at), (shards_of,), jnp.float32, low / len(cuts), high / len(cuts))
        factor_of = factor_of * jnp.repeat(jnp.exp(heights), extent[axis_at] // shards_of).reshape((-1,) + (1,) * (len(extent) - 1 - axis_at))
    return factor_of


def gaussian(key, dims, width, most, cuts=(), dtype=jnp.bfloat16):
    entries = jax.random.normal(key, dims, jnp.float32) * width
    if len(cuts) > 0:
        entries = block_scale(key, dims, cuts, -0.22, 0.18) * entries
    return jnp.clip(entries, min=-most, max=most).astype(dtype)


def setup_inputs(seed: int = 0, part: int = 0) -> dict:
    seeds = jax.random.split(jax.random.key(seed), 15)
    part_keys = jax.random.split(jax.random.fold_in(seeds[14], part), 15)
    return {
        "token_ids": place_ends(jax.random.randint(part_keys[0], (MB_TOK, MICRO), 0, VOCAB), jax.random.fold_in(part_keys[0], 1), 0, VOCAB - 1).astype(jnp.int32),
        "lengths": draw_lengths(jax.random.fold_in(jax.random.fold_in(seeds[14], part), 71), part),
        "embed_table": gaussian(seeds[2], (VOCAB, D), 1.0, 6.0),
        "gain_attn": jnp.clip(1.0 + 0.18 * jax.random.normal(seeds[3], (D,), jnp.float32), 0.1, 1.9),
        "w_qkv": gaussian(seeds[4], (D, 3 * D), D ** -0.5, 0.078125, ((1, 16),)),
        "w_out": gaussian(seeds[5], (D, D), D ** -0.5, 0.078125, ((1, 16),)),
        "gain_first": jnp.clip(1.0 + 0.18 * jax.random.normal(seeds[6], (D,), jnp.float32), 0.1, 1.9),
        "gate_first": gaussian(seeds[7], (D, FFW), D ** -0.5, 0.078125, ((1, 16),)),
        "up_first": gaussian(seeds[8], (D, FFW), D ** -0.5, 0.078125, ((1, 16),)),
        "down_first": gaussian(seeds[9], (FFW, D), (FFW // 4) ** -0.5, 0.09375, ((0, 16),)),
        "gain_second": jnp.clip(1.0 + 0.18 * jax.random.normal(seeds[10], (D,), jnp.float32), 0.1, 1.9),
        "gate_second": gaussian(seeds[11], (D, FFW), D ** -0.5, 0.078125, ((1, 16),)),
        "up_second": gaussian(seeds[12], (D, FFW), D ** -0.5, 0.078125, ((1, 16),)),
        "down_second": gaussian(seeds[13], (FFW, D), (FFW // 4) ** -0.5, 0.09375, ((0, 16),)),
    }


def norm_rows(values, gain_vec):
    row_mean = lax.optimization_barrier(jnp.mean(values, axis=-1, keepdims=True))
    centred = values - row_mean
    row_var = lax.optimization_barrier(jnp.mean(centred * centred, axis=-1, keepdims=True))
    return (centred * lax.rsqrt(row_var + 1e-05) * gain_vec).astype(jnp.bfloat16)

def project(inputs, weight_mat):
    return jnp.einsum('pmd,dc->pmc', inputs.astype(jnp.float32), weight_mat.astype(jnp.float32))

def feed_forward(resid, gain_vec, gate_mat, up_mat, down_mat):
    normed = norm_rows(resid, gain_vec)
    hidden = (jax.nn.silu(project(normed, gate_mat)) * project(normed, up_mat)).astype(jnp.bfloat16)
    return resid + project(hidden, down_mat)

def reference(token_ids, lengths, embed_table, gain_attn, w_qkv, w_out, gain_first, gate_first, up_first, down_first, gain_second, gate_second, up_second, down_second):
    embedded = embed_table[token_ids].astype(jnp.float32)
    normed_attn = norm_rows(embedded, gain_attn)
    projected = project(normed_attn, w_qkv).astype(jnp.bfloat16)
    queries = projected[..., :D].reshape(MB_TOK, MICRO, H, HD).astype(jnp.float32)
    key_rows = projected[..., D:2 * D].reshape(MB_TOK, MICRO, H, HD).astype(jnp.float32)
    value_rows = projected[..., 2 * D:].reshape(MB_TOK, MICRO, H, HD).astype(jnp.float32)
    scores = jnp.einsum('pmhe,qmhe->pmhq', queries, key_rows) * HD ** (-0.5)
    live_keys = (jnp.arange(MB_TOK)[None, :] < lengths[:, None]).astype(jnp.float32)
    weights = jnp.exp(scores) * live_keys[None, :, None, :]
    denominator = lax.optimization_barrier(jnp.sum(weights, axis=-1))
    numerator = jnp.einsum('pmhq,qmhe->pmhe', weights.astype(jnp.bfloat16).astype(jnp.float32), value_rows)
    attended = (numerator / denominator[..., None]).reshape(MB_TOK, MICRO, D).astype(jnp.bfloat16)
    attn_proj = project(attended, w_out).astype(jnp.bfloat16)
    after_attn = embedded + attn_proj.astype(jnp.float32)
    after_first = feed_forward(after_attn, gain_first, gate_first, up_first, down_first)
    after_second = feed_forward(after_first, gain_second, gate_second, up_second, down_second)
    return after_second.astype(jnp.bfloat16)
```

```python
import functools
import math

import jax
import jax.numpy as jnp
from jax import lax
from jax.experimental import pallas as pl
from jax.experimental.pallas import tpu as pltpu
from jax.sharding import PartitionSpec as P

H = 48
HD = 128
F32 = jnp.float32
BF16 = jnp.bfloat16
VM = pl.BlockSpec(memory_space=pltpu.VMEM)
SM = pl.BlockSpec(memory_space=pltpu.SMEM)
HB = pl.BlockSpec(memory_space=pltpu.HBM)


def norm_rows(values, gain_vec):
    row_mean = jnp.mean(values, axis=-1, keepdims=True)
    centred = values - row_mean
    row_var = jnp.mean(centred * centred, axis=-1, keepdims=True)
    return (centred * lax.rsqrt(row_var + 1e-05) * gain_vec).astype(jnp.bfloat16)


def local_hidden(normed, gate_mat, up_mat):
    gated = jnp.einsum("pmd,dc->pmc", normed, gate_mat, preferred_element_type=jnp.float32)
    lifted = jnp.einsum("pmd,dc->pmc", normed, up_mat, preferred_element_type=jnp.float32)
    return (jax.nn.silu(gated) * lifted).astype(jnp.bfloat16)


def spread_rows(local_rows, row_fn):
    return row_fn(lax.all_gather(local_rows, "tensor", axis=0, tiled=True), jnp.int32(0))


def to_tokens(columns):
    return lax.all_to_all(columns, "tensor", split_axis=0, concat_axis=2, tiled=True)


def down_sum(hidden_all, down_mat):
    return lax.psum_scatter(
        jnp.einsum("pmc,cd->pmd", hidden_all, down_mat, preferred_element_type=jnp.float32),
        "tensor",
        scatter_dimension=0,
        tiled=True,
    )


def local(
    token_ids,
    lengths,
    embed_table,
    gain_attn,
    w_qkv,
    w_out,
    gain_first,
    gate_first,
    up_first,
    down_first,
    gain_second,
    gate_second,
    up_second,
    down_second,
):
    rows_here = token_ids.shape[0]
    micro_count = token_ids.shape[1]
    vocab_size = embed_table.shape[0]
    own_start = lax.axis_index("tensor") * rows_here
    onehot = (token_ids[:, :, None] == jnp.arange(vocab_size)[None, None, :]).astype(jnp.bfloat16)
    embedded = jnp.einsum("pmv,vd->pmd", onehot, embed_table, preferred_element_type=jnp.float32)
    normed_attn = norm_rows(embedded, gain_attn)

    def qkv_rows(row_piece, row_start):
        return jnp.einsum(
            "pmd,dc->pmc", row_piece, w_qkv, preferred_element_type=jnp.float32
        ).astype(jnp.bfloat16)

    projected = to_tokens(spread_rows(normed_attn, qkv_rows))
    feat_width = projected.shape[2] // 3
    queries = projected[..., :feat_width].reshape(rows_here, micro_count, H, HD)
    key_rows = projected[..., feat_width : 2 * feat_width]
    value_rows = projected[..., 2 * feat_width :]
    score_scale = HD ** (-0.5)
    key_piece = lax.all_gather(key_rows, "tensor", axis=0, tiled=True)
    value_piece = lax.all_gather(value_rows, "tensor", axis=0, tiled=True)
    piece_rows = key_piece.shape[0]
    key_heads = key_piece.reshape(piece_rows, micro_count, H, HD)
    value_heads = value_piece.reshape(piece_rows, micro_count, H, HD)
    scores = (
        jnp.einsum("pmhe,qmhe->pmhq", queries, key_heads, preferred_element_type=jnp.float32)
        * score_scale
    )
    positions = jnp.arange(piece_rows)
    live_keys = (positions[None, :] < lengths[:, None]).astype(jnp.float32)
    weights = jnp.exp(scores) * live_keys[None, :, None, :]
    denominator = jnp.sum(weights, axis=-1)
    numerator = jnp.einsum(
        "pmhq,qmhe->pmhe",
        weights.astype(jnp.bfloat16),
        value_heads,
        preferred_element_type=jnp.float32,
    )
    numerator, denominator = (numerator, denominator)
    attended = (
        (numerator / denominator[..., None])
        .reshape(rows_here, micro_count, feat_width)
        .astype(jnp.bfloat16)
    )

    def out_rows(row_piece, row_start):
        return jnp.einsum(
            "pmd,dc->pmc", row_piece, w_out, preferred_element_type=jnp.float32
        ).astype(jnp.bfloat16)

    after_attn = embedded + to_tokens(spread_rows(attended, out_rows)).astype(jnp.float32)

    def first_rows(row_piece, row_start):
        return local_hidden(row_piece, gate_first, up_first)

    hidden_first = spread_rows(norm_rows(after_attn, gain_first), first_rows)
    partial_all = jnp.einsum(
        "pmc,cd->pmd", hidden_first, down_first, preferred_element_type=jnp.float32
    )
    own_rows = lax.dynamic_slice_in_dim(partial_all, own_start, rows_here, 0) + after_attn
    partial_all = lax.dynamic_update_slice_in_dim(partial_all, own_rows, own_start, 0)
    first_all = lax.psum(partial_all, "tensor")
    after_first = lax.dynamic_slice_in_dim(first_all, own_start, rows_here, 0)
    hidden_second = local_hidden(norm_rows(first_all, gain_second), gate_second, up_second)
    after_second = after_first + down_sum(hidden_second, down_second)
    return after_second.astype(jnp.bfloat16)


def dot(a, b):
    return jnp.dot(a, b, preferred_element_type=F32)


def in_vmem(x):
    return pltpu.with_memory_space_constraint(x, pltpu.VMEM)


def call(body, out_shape, args, specs, flops, limit_mib, scratch=()):
    many = isinstance(out_shape, (tuple, list))
    return pl.pallas_call(
        body,
        out_shape=out_shape,
        in_specs=specs,
        out_specs=[VM] * len(out_shape) if many else VM,
        scratch_shapes=list(scratch),
        compiler_params=pltpu.CompilerParams(vmem_limit_bytes=limit_mib << 20),
        cost_estimate=pl.CostEstimate(flops=int(flops), transcendentals=0, bytes_accessed=1 << 20),
    )(*args)


def project_body(pieces, onehot_ref, table_ref, gain_ref, w_hbm, q_ref, k_ref, v_ref, w_buf, normed, sems):
    depth = w_hbm.shape[0] // pieces
    copies = [
        pltpu.make_async_copy(
            w_hbm.at[pl.ds(i * depth, depth)], w_buf.at[pl.ds(i * depth, depth)], sems.at[i]
        )
        for i in range(pieces)
    ]
    for one in copies:
        one.start()
    values = table_ref[...].astype(F32)
    centred = values - jnp.mean(values, axis=-1, keepdims=True)
    var = jnp.mean(centred * centred, axis=-1, keepdims=True)
    normed[...] = (centred * lax.rsqrt(var + 1e-05) * gain_ref[...]).astype(BF16)
    total = jnp.zeros((normed.shape[0], w_hbm.shape[1]), F32)
    for i, one in enumerate(copies):
        one.wait()
        total += dot(normed[:, i * depth : (i + 1) * depth], w_buf[i * depth : (i + 1) * depth, :])
    rows = dot(onehot_ref[...], total.astype(BF16)).astype(BF16)
    width = q_ref.shape[1]
    q_ref[...] = rows[:, :width]
    k_ref[...] = rows[:, width : 2 * width]
    v_ref[...] = rows[:, 2 * width :]


def attend_body(n, micro, lens_ref, r0_ref, r1_ref, r2_ref, out_ref):
    me = lax.axis_index("tensor")
    got = (r0_ref[...], r1_ref[...], r2_ref[...])

    def block(b):
        at = lax.rem(me + b * n, 3)
        return jnp.where(at == 0, got[0], jnp.where(at == 1, got[1], got[2]))

    queries, keys, values = block(0), block(1), block(2)
    rows, width = queries.shape
    row_at = lax.broadcasted_iota(jnp.int32, (rows, rows), 0)
    key_at = lax.broadcasted_iota(jnp.int32, (rows, rows), 1)
    live = jnp.zeros((rows, rows), jnp.bool_)
    for m in range(micro):
        both = (row_at % micro == m) & (key_at % micro == m)
        live = live | (both & (key_at // micro < lens_ref[m]))
    for h in range(width // HD):
        cols = slice(h * HD, (h + 1) * HD)
        scores = lax.dot_general(
            queries[:, cols], keys[:, cols], (((1,), (1,)), ((), ())), preferred_element_type=F32
        ) * (HD ** (-0.5))
        weights = jnp.where(live, jnp.exp(scores), 0.0)
        denominator = jnp.sum(weights, axis=-1, keepdims=True)
        numerator = dot(weights.astype(BF16), values[:, cols])
        attended = (numerator / denominator).astype(BF16)
        for e in range(out_ref.shape[0]):
            out_ref[e, :, cols] = attended


def out_body(own_ref, oth_ref, w_ref, onehot_ref, table_ref, send_ref, resid_ref):
    me = lax.axis_index("tensor")
    core = lax.rem(me, 2)
    chips, rows, width = own_ref.shape
    total = jnp.zeros((rows, width), F32)
    for e in range(chips):
        for ref, c in ((own_ref, core), (oth_ref, 1 - core)):
            at = pl.multiple_of((2 * e + c) * width, 128)
            total += dot(ref[e], w_ref[pl.ds(at, width), :])
    here = pl.multiple_of(me * width, 128)
    embedded = dot(onehot_ref[...], table_ref[:, pl.ds(here, width)])
    after = embedded + total.astype(BF16).astype(F32)
    resid_ref[...] = after
    for e in range(chips):
        send_ref[e] = after.astype(BF16)


def hidden_body(own_ref, oth_ref, gain_ref, g_ref, u_ref, h_ref, normed):
    core = lax.rem(lax.axis_index("tensor"), 2)
    chips, rows, width = own_ref.shape
    own, oth = own_ref[...].astype(F32), oth_ref[...].astype(F32)
    count = 2 * chips * width

    def row_sum(a, b):
        return jnp.sum(jnp.sum(a + b, axis=0), axis=-1, keepdims=True)

    mean = row_sum(own, oth) / count
    own, oth = own - mean[None], oth - mean[None]
    scale = lax.rsqrt(row_sum(own * own, oth * oth) / count + 1e-05)
    for e in range(chips):
        for x, c in ((own, core), (oth, 1 - core)):
            at = pl.ds(pl.multiple_of((2 * e + c) * width, 128), width)
            normed[:, at] = (x[e] * scale * gain_ref[:, at]).astype(BF16)
    step = 256
    for j in range(0, g_ref.shape[1], step):
        gated = dot(normed[...], g_ref[:, j : j + step])
        lifted = dot(normed[...], u_ref[:, j : j + step])
        h_ref[:, j : j + step] = (jax.nn.silu(gated) * lifted).astype(BF16)


def down_body(h_ref, d_ref, keep_ref, send_ref):
    core = lax.rem(lax.axis_index("tensor"), 2)
    chips, rows, width = keep_ref.shape
    for ref, c in ((send_ref, 1 - core), (keep_ref, core)):
        for e in range(chips):
            at = pl.multiple_of((2 * e + c) * width, 128)
            ref[e] = dot(h_ref[...], d_ref[:, pl.ds(at, width)]).astype(BF16)


def add_body(a_ref, b_ref, out_ref):
    out_ref[...] = (a_ref[...].astype(F32) + b_ref[...].astype(F32)).astype(BF16)


def settle_body(got_ref, resid_ref, send_ref, after_ref):
    after = resid_ref[...] + jnp.sum(got_ref[...].astype(F32), axis=0)
    after_ref[...] = after
    for e in range(send_ref.shape[0]):
        send_ref[e] = after.astype(BF16)


def last_body(h_ref, d_ref, resid_ref, out_ref):
    me = lax.axis_index("tensor")
    rows, width = resid_ref.shape
    for k in range(d_ref.shape[1] // width):
        cols = slice(k * width, (k + 1) * width)
        part = dot(h_ref[...], d_ref[:, cols])
        out_ref[:, cols] = (part + jnp.where(me == k, resid_ref[...], 0.0)).astype(BF16)


def final_body(got_ref, out_ref):
    out_ref[...] = jnp.sum(got_ref[...].astype(F32), axis=0, keepdims=True).astype(BF16)


FLOPS = {"project": 1e9, "attend": 1e9, "out": 1e9, "hidden": 1e9, "down": 1e9, "add": 1e9, "settle": 1e9}


def fast_local(
    n,
    token_ids,
    lengths,
    embed_table,
    gain_attn,
    w_qkv,
    w_out,
    gain_first,
    gate_first,
    up_first,
    down_first,
    gain_second,
    gate_second,
    up_second,
    down_second,
):
    rows_here, micro = token_ids.shape
    rows = n * rows_here * micro
    vocab, width = embed_table.shape
    chips = n // 2
    part = width // n
    same_core = [[2 * e + c for e in range(chips)] for c in range(2)]

    def exchange(x):
        return lax.all_to_all(x, "tensor", 0, 0, tiled=True, axis_index_groups=same_core)

    def partner(x):
        return lax.ppermute(x, "tensor", [(i, i ^ 1) for i in range(n)])

    def shape(dims, dtype=BF16):
        return jax.ShapeDtypeStruct(dims, dtype)

    all_ids = lax.all_to_all(
        jnp.broadcast_to(token_ids[None], (n, rows_here, micro)), "tensor", 0, 0, tiled=True
    )
    onehot = (all_ids.reshape(rows, 1) == jnp.arange(vocab)[None, :]).astype(BF16)

    pieces = 12
    triples = call(
        functools.partial(project_body, pieces),
        [shape((rows, part))] * 3,
        (onehot, embed_table, gain_attn[None], pltpu.with_memory_space_constraint(w_qkv, pltpu.HBM)),
        [VM, VM, VM, HB],
        FLOPS["project"],
        24,
        [
            pltpu.VMEM(w_qkv.shape, BF16),
            pltpu.VMEM((vocab, width), BF16),
            pltpu.SemaphoreType.DMA((pieces,)),
        ],
    )
    got = [
        lax.ppermute(triples[i], "tensor", [(d, (3 * d + i) % n) for d in range(n)]) for i in range(3)
    ]
    share = shape((chips, rows, part))
    attended = call(
        functools.partial(attend_body, n, micro), share, (lengths, *got), [SM, VM, VM, VM], FLOPS["attend"], 2
    )
    own = exchange(attended)
    after_send, resid = call(
        out_body,
        (share, shape((rows, part), F32)),
        (own, partner(own), in_vmem(w_out), onehot, embed_table),
        [VM] * 5,
        FLOPS["out"],
        2,
    )

    def hidden_of(sent, gain, gate, up):
        own = exchange(sent)
        return call(
            hidden_body,
            shape((rows, gate.shape[1])),
            (own, partner(own), gain[None], in_vmem(gate), in_vmem(up)),
            [VM] * 5,
            FLOPS["hidden"],
            4,
            [pltpu.VMEM((rows, width), BF16)],
        )

    hidden = hidden_of(after_send, gain_first, gate_first, up_first)
    keep, send = call(down_body, (share, share), (hidden, in_vmem(down_first)), [VM] * 2, FLOPS["down"], 2)
    summed = call(add_body, share, (keep, partner(send)), [VM] * 2, FLOPS["add"], 2)
    first_send, resid = call(
        settle_body, (share, shape((rows, part), F32)), (exchange(summed), resid), [VM] * 2, FLOPS["settle"], 2
    )
    hidden = hidden_of(first_send, gain_second, gate_second, up_second)
    partial_all = call(last_body, shape((rows, width)), (hidden, in_vmem(down_second), resid), [VM] * 3, 1e9, 2)
    core = lax.axis_index("tensor") % 2
    halves = partial_all.reshape(chips, 2, rows_here * micro, width)
    keep = lax.dynamic_index_in_dim(halves, core, 1, keepdims=False)
    send = lax.dynamic_index_in_dim(halves, 1 - core, 1, keepdims=False)
    summed = (keep.astype(F32) + partner(send).astype(F32)).astype(BF16)
    landed = exchange(summed)
    out = jnp.sum(landed.astype(F32), axis=0).astype(BF16)
    return out.reshape(rows_here, micro, width)


def pick(mesh):
    n = mesh.shape["tensor"]
    if n % 2 == 0 and H % n == 0 and math.gcd(n, 3) == 1:
        return functools.partial(fast_local, n)
    return local


def solution(mesh):
    return jax.shard_map(
        pick(mesh),
        mesh=mesh,
        in_specs=(
            P("tensor", "groups"),
            P("groups"),
            P(),
            P(),
            P(None, "tensor"),
            P(None, "tensor"),
            P(),
            P(None, "tensor"),
            P(None, "tensor"),
            P("tensor", None),
            P(),
            P(None, "tensor"),
            P(None, "tensor"),
            P("tensor", None),
        ),
        out_specs=P("tensor", "groups", None),
        check_vma=False,
    )
```

```python
import functools
import math

import jax
import jax.numpy as jnp
from jax import lax
from jax.experimental import pallas as pl
from jax.experimental.pallas import tpu as pltpu
from jax.sharding import PartitionSpec as P

H = 48
HD = 128
F32 = jnp.float32
BF16 = jnp.bfloat16
VM = pl.BlockSpec(memory_space=pltpu.VMEM)
SM = pl.BlockSpec(memory_space=pltpu.SMEM)
HB = pl.BlockSpec(memory_space=pltpu.HBM)


def norm_rows(values, gain_vec):
    row_mean = jnp.mean(values, axis=-1, keepdims=True)
    centred = values - row_mean
    row_var = jnp.mean(centred * centred, axis=-1, keepdims=True)
    return (centred * lax.rsqrt(row_var + 1e-05) * gain_vec).astype(jnp.bfloat16)


def local_hidden(normed, gate_mat, up_mat):
    gated = jnp.einsum("pmd,dc->pmc", normed, gate_mat, preferred_element_type=jnp.float32)
    lifted = jnp.einsum("pmd,dc->pmc", normed, up_mat, preferred_element_type=jnp.float32)
    return (jax.nn.silu(gated) * lifted).astype(jnp.bfloat16)


def spread_rows(local_rows, row_fn):
    return row_fn(lax.all_gather(local_rows, "tensor", axis=0, tiled=True), jnp.int32(0))


def to_tokens(columns):
    return lax.all_to_all(columns, "tensor", split_axis=0, concat_axis=2, tiled=True)


def down_sum(hidden_all, down_mat):
    return lax.psum_scatter(
        jnp.einsum("pmc,cd->pmd", hidden_all, down_mat, preferred_element_type=jnp.float32),
        "tensor",
        scatter_dimension=0,
        tiled=True,
    )


def local(
    token_ids,
    lengths,
    embed_table,
    gain_attn,
    w_qkv,
    w_out,
    gain_first,
    gate_first,
    up_first,
    down_first,
    gain_second,
    gate_second,
    up_second,
    down_second,
):
    rows_here = token_ids.shape[0]
    micro_count = token_ids.shape[1]
    vocab_size = embed_table.shape[0]
    own_start = lax.axis_index("tensor") * rows_here
    onehot = (token_ids[:, :, None] == jnp.arange(vocab_size)[None, None, :]).astype(jnp.bfloat16)
    embedded = jnp.einsum("pmv,vd->pmd", onehot, embed_table, preferred_element_type=jnp.float32)
    normed_attn = norm_rows(embedded, gain_attn)

    def qkv_rows(row_piece, row_start):
        return jnp.einsum(
            "pmd,dc->pmc", row_piece, w_qkv, preferred_element_type=jnp.float32
        ).astype(jnp.bfloat16)

    projected = to_tokens(spread_rows(normed_attn, qkv_rows))
    feat_width = projected.shape[2] // 3
    queries = projected[..., :feat_width].reshape(rows_here, micro_count, H, HD)
    key_rows = projected[..., feat_width : 2 * feat_width]
    value_rows = projected[..., 2 * feat_width :]
    score_scale = HD ** (-0.5)
    key_piece = lax.all_gather(key_rows, "tensor", axis=0, tiled=True)
    value_piece = lax.all_gather(value_rows, "tensor", axis=0, tiled=True)
    piece_rows = key_piece.shape[0]
    key_heads = key_piece.reshape(piece_rows, micro_count, H, HD)
    value_heads = value_piece.reshape(piece_rows, micro_count, H, HD)
    scores = (
        jnp.einsum("pmhe,qmhe->pmhq", queries, key_heads, preferred_element_type=jnp.float32)
        * score_scale
    )
    positions = jnp.arange(piece_rows)
    live_keys = (positions[None, :] < lengths[:, None]).astype(jnp.float32)
    weights = jnp.exp(scores) * live_keys[None, :, None, :]
    denominator = jnp.sum(weights, axis=-1)
    numerator = jnp.einsum(
        "pmhq,qmhe->pmhe",
        weights.astype(jnp.bfloat16),
        value_heads,
        preferred_element_type=jnp.float32,
    )
    numerator, denominator = (numerator, denominator)
    attended = (
        (numerator / denominator[..., None])
        .reshape(rows_here, micro_count, feat_width)
        .astype(jnp.bfloat16)
    )

    def out_rows(row_piece, row_start):
        return jnp.einsum(
            "pmd,dc->pmc", row_piece, w_out, preferred_element_type=jnp.float32
        ).astype(jnp.bfloat16)

    after_attn = embedded + to_tokens(spread_rows(attended, out_rows)).astype(jnp.float32)

    def first_rows(row_piece, row_start):
        return local_hidden(row_piece, gate_first, up_first)

    hidden_first = spread_rows(norm_rows(after_attn, gain_first), first_rows)
    partial_all = jnp.einsum(
        "pmc,cd->pmd", hidden_first, down_first, preferred_element_type=jnp.float32
    )
    own_rows = lax.dynamic_slice_in_dim(partial_all, own_start, rows_here, 0) + after_attn
    partial_all = lax.dynamic_update_slice_in_dim(partial_all, own_rows, own_start, 0)
    first_all = lax.psum(partial_all, "tensor")
    after_first = lax.dynamic_slice_in_dim(first_all, own_start, rows_here, 0)
    hidden_second = local_hidden(norm_rows(first_all, gain_second), gate_second, up_second)
    after_second = after_first + down_sum(hidden_second, down_second)
    return after_second.astype(jnp.bfloat16)


def dot(a, b):
    return jnp.dot(a, b, preferred_element_type=F32)


def in_vmem(x):
    return pltpu.with_memory_space_constraint(x, pltpu.VMEM)


def call(body, out_shape, args, specs, flops, limit_mib, scratch=()):
    many = isinstance(out_shape, (tuple, list))
    return pl.pallas_call(
        body,
        out_shape=out_shape,
        in_specs=specs,
        out_specs=[VM] * len(out_shape) if many else VM,
        scratch_shapes=list(scratch),
        compiler_params=pltpu.CompilerParams(vmem_limit_bytes=limit_mib << 20),
        cost_estimate=pl.CostEstimate(flops=int(flops), transcendentals=0, bytes_accessed=1 << 20),
    )(*args)


def mark_body(ids_ref, hot_ref):
    copies, height, lanes = hot_ref.shape
    rows_here, micro = ids_ref.shape
    row_at = lax.broadcasted_iota(jnp.int32, (height, lanes), 0)
    word_at = lax.broadcasted_iota(jnp.int32, (height, lanes), 1)
    hot = jnp.zeros((height, lanes), F32)
    for p in range(rows_here):
        for m in range(micro):
            here = (row_at == p * micro + m) & (word_at == ids_ref[p, m])
            hot = jnp.where(here, 1.0, hot)
    for i in range(copies):
        hot_ref[i] = hot


def project_body(pieces, table_hbm, gain_hbm, w_hbm, rows_ref, cols_ref, table, gain, w_buf, normed, sems, w_sems):
    me = lax.axis_index("tensor")
    depth = w_hbm.shape[0] // pieces
    small = [
        pltpu.make_async_copy(table_hbm, table, sems.at[0]),
        pltpu.make_async_copy(gain_hbm, gain, sems.at[1]),
    ]
    copies = [
        pltpu.make_async_copy(
            w_hbm.at[pl.ds(i * depth, depth)], w_buf.at[pl.ds(i * depth, depth)], w_sems.at[i]
        )
        for i in range(pieces)
    ]
    for one in small + copies:
        one.start()
    for one in small:
        one.wait()
    values = table[...].astype(F32)
    centred = values - jnp.mean(values, axis=-1, keepdims=True)
    var = jnp.mean(centred * centred, axis=-1, keepdims=True)
    normed[...] = (centred * lax.rsqrt(var + 1e-05) * gain[...]).astype(BF16)
    width = cols_ref.shape[1]
    cols_ref[...] = table[:, pl.ds(pl.multiple_of(me * width, 128), width)]
    total = jnp.zeros((normed.shape[0], w_hbm.shape[1]), F32)
    for i, one in enumerate(copies):
        one.wait()
        total += dot(normed[:, i * depth : (i + 1) * depth], w_buf[i * depth : (i + 1) * depth, :])
    rows_ref[...] = total.astype(BF16)


def choose_body(rm, hot_ref, rows_ref, cols_ref, t0_ref, t1_ref, t2_ref, emb_ref):
    vocab = rows_ref.shape[0]
    onehot = jnp.concatenate([hot_ref[p, :rm, :vocab] for p in range(hot_ref.shape[0])], axis=0).astype(BF16)
    width = t0_ref.shape[1]
    for i, ref in enumerate((t0_ref, t1_ref, t2_ref)):
        ref[...] = dot(onehot, rows_ref[:, i * width : (i + 1) * width]).astype(BF16)
    emb_ref[...] = dot(onehot, cols_ref[...])


def owned(n, d):
    return lax.rem(3 * d + 1, n)


def attend_body(n, micro, lens_ref, r0_ref, r1_ref, r2_ref, out_ref):
    head = owned(n, lax.axis_index("tensor"))
    got = (r0_ref[...], r1_ref[...], r2_ref[...])

    def block(b):
        at = lax.rem(head + b * n, 3)
        return jnp.where(at == 0, got[0], jnp.where(at == 1, got[1], got[2]))

    queries, keys, values = block(0), block(1), block(2)
    rows, width = queries.shape
    row_at = lax.broadcasted_iota(jnp.int32, (rows, rows), 0)
    key_at = lax.broadcasted_iota(jnp.int32, (rows, rows), 1)
    live = jnp.zeros((rows, rows), jnp.bool_)
    for m in range(micro):
        both = (row_at % micro == m) & (key_at % micro == m)
        live = live | (both & (key_at // micro < lens_ref[m]))
    for h in range(width // HD):
        cols = slice(h * HD, (h + 1) * HD)
        scores = lax.dot_general(
            queries[:, cols], keys[:, cols], (((1,), (1,)), ((), ())), preferred_element_type=F32
        ) * (HD ** (-0.5))
        weights = jnp.where(live, jnp.exp(scores), 0.0)
        denominator = jnp.sum(weights, axis=-1, keepdims=True)
        numerator = dot(weights.astype(BF16), values[:, cols])
        attended = (numerator / denominator).astype(BF16)
        for e in range(out_ref.shape[0]):
            out_ref[e, :, cols] = attended


def out_sum(n, ref, c, w_ref):
    chips, rows, width = ref.shape
    total = jnp.zeros((rows, width), F32)
    for e in range(chips):
        at = pl.multiple_of(owned(n, 2 * e + c) * width, 128)
        total += dot(ref[e], w_ref[pl.ds(at, width), :])
    return total


def out_own_body(n, own_ref, w_ref, total_ref):
    core = lax.rem(lax.axis_index("tensor"), 2)
    total_ref[...] = out_sum(n, own_ref, core, w_ref)


def out_oth_body(n, oth_ref, w_ref, total_ref, emb_ref, send_ref, resid_ref):
    core = lax.rem(lax.axis_index("tensor"), 2)
    total = total_ref[...] + out_sum(n, oth_ref, 1 - core, w_ref)
    after = emb_ref[...] + total.astype(BF16).astype(F32)
    resid_ref[...] = after
    for e in range(send_ref.shape[0]):
        send_ref[e] = after.astype(BF16)


def hidden_body(own_ref, oth_ref, gain_ref, g_ref, u_ref, h_ref, normed):
    core = lax.rem(lax.axis_index("tensor"), 2)
    chips, rows, width = own_ref.shape
    own, oth = own_ref[...].astype(F32), oth_ref[...].astype(F32)
    count = 2 * chips * width

    def row_sum(a, b):
        return jnp.sum(jnp.sum(a + b, axis=0), axis=-1, keepdims=True)

    mean = row_sum(own, oth) / count
    own, oth = own - mean[None], oth - mean[None]
    scale = lax.rsqrt(row_sum(own * own, oth * oth) / count + 1e-05)
    for e in range(chips):
        for x, c in ((own, core), (oth, 1 - core)):
            at = pl.ds(pl.multiple_of((2 * e + c) * width, 128), width)
            normed[:, at] = (x[e] * scale * gain_ref[:, at]).astype(BF16)
    step = 256
    for j in range(0, g_ref.shape[1], step):
        gated = dot(normed[...], g_ref[:, j : j + step])
        lifted = dot(normed[...], u_ref[:, j : j + step])
        h_ref[:, j : j + step] = (jax.nn.silu(gated) * lifted).astype(BF16)


def down_body(other, h_ref, d_ref, out_ref):
    core = lax.rem(lax.axis_index("tensor") + other, 2)
    chips, rows, width = out_ref.shape
    for e in range(chips):
        at = pl.multiple_of((2 * e + core) * width, 128)
        out_ref[e] = dot(h_ref[...], d_ref[:, pl.ds(at, width)]).astype(BF16)


def add_body(a_ref, b_ref, out_ref):
    out_ref[...] = (a_ref[...].astype(F32) + b_ref[...].astype(F32)).astype(BF16)


def settle_body(got_ref, resid_ref, send_ref, after_ref):
    after = resid_ref[...] + jnp.sum(got_ref[...].astype(F32), axis=0)
    after_ref[...] = after
    for e in range(send_ref.shape[0]):
        send_ref[e] = after.astype(BF16)


def last_body(h_ref, d_ref, resid_ref, keep_ref, send_ref):
    me = lax.axis_index("tensor")
    core = lax.rem(me, 2)
    chips, rm, _ = keep_ref.shape
    rows, width = resid_ref.shape
    half = rows // 2
    to = lax.broadcasted_iota(jnp.int32, (rows, rows), 0)
    at = lax.broadcasted_iota(jnp.int32, (rows, rows), 1)
    rest = to % half
    side = jnp.where(to < half, core, 1 - core)
    moved = at == (2 * (rest // rm) + side) * rm + rest % rm
    hidden = dot(moved.astype(BF16), h_ref[...]).astype(BF16)
    resid = jnp.dot(
        moved.astype(F32), resid_ref[...], precision=lax.Precision.HIGHEST, preferred_element_type=F32
    )
    for k in range(d_ref.shape[1] // width):
        cols = slice(k * width, (k + 1) * width)
        part = dot(hidden, d_ref[:, cols]) + jnp.where(me == k, resid, 0.0)
        for e in range(chips):
            keep_ref[e, :, cols] = part[e * rm : (e + 1) * rm].astype(BF16)
            send_ref[e, :, cols] = part[half + e * rm : half + (e + 1) * rm].astype(BF16)


def final_body(got_ref, out_ref):
    out_ref[...] = jnp.sum(got_ref[...].astype(F32), axis=0).astype(BF16)


FLOPS = {
    "mark": 1e9,
    "project": 5e10,
    "choose": 1e10,
    "attend": 1e10,
    "out": 3e9,
    "hidden": 5e9,
    "down": 5e10,
    "add": 5e10,
    "settle": 5e10,
}


def fast_local(
    n,
    token_ids,
    lengths,
    embed_table,
    gain_attn,
    w_qkv,
    w_out,
    gain_first,
    gate_first,
    up_first,
    down_first,
    gain_second,
    gate_second,
    up_second,
    down_second,
):
    rows_here, micro = token_ids.shape
    rows = n * rows_here * micro
    vocab, width = embed_table.shape
    chips = n // 2
    part = width // n
    same_core = [[2 * e + c for e in range(chips)] for c in range(2)]

    def exchange(x):
        return lax.all_to_all(x, "tensor", 0, 0, tiled=True, axis_index_groups=same_core)

    def partner(x):
        return lax.ppermute(x, "tensor", [(i, i ^ 1) for i in range(n)])

    def shape(dims, dtype=BF16):
        return jax.ShapeDtypeStruct(dims, dtype)

    rm = rows_here * micro
    marks = call(
        mark_body, shape((n, -(-rm // 8) * 8, -(-vocab // 128) * 128), F32), (token_ids,), [SM], FLOPS["mark"], 2
    )
    hot = lax.all_to_all(marks, "tensor", 0, 0, tiled=True)
    pieces = 12
    far = [pltpu.with_memory_space_constraint(x, pltpu.HBM) for x in (embed_table, gain_attn[None], w_qkv)]
    table_rows, table_cols = call(
        functools.partial(project_body, pieces),
        (shape((vocab, w_qkv.shape[1])), shape((vocab, part))),
        far,
        [HB] * 3,
        FLOPS["project"],
        24,
        [
            pltpu.VMEM(embed_table.shape, BF16),
            pltpu.VMEM((1, width), F32),
            pltpu.VMEM(w_qkv.shape, BF16),
            pltpu.VMEM((vocab, width), BF16),
            pltpu.SemaphoreType.DMA((2,)),
            pltpu.SemaphoreType.DMA((pieces,)),
        ],
    )
    triples = call(
        functools.partial(choose_body, rm),
        [shape((rows, part))] * 3 + [shape((rows, part), F32)],
        (hot, table_rows, table_cols),
        [VM] * 3,
        FLOPS["choose"],
        2,
    )
    turn = pow(3, -1, n)
    got = [
        lax.ppermute(triples[0], "tensor", [(d, (d - turn) % n) for d in range(n)]),
        triples[1],
        lax.ppermute(triples[2], "tensor", [(d, (d + turn) % n) for d in range(n)]),
    ]
    share = shape((chips, rows, part))
    attended = call(
        functools.partial(attend_body, n, micro), share, (lengths, *got), [SM, VM, VM, VM], FLOPS["attend"], 2
    )
    own = exchange(attended)
    w_near = in_vmem(w_out)
    total = call(
        functools.partial(out_own_body, n), shape((rows, part), F32), (own, w_near), [VM] * 2, FLOPS["out"], 2
    )
    after_send, resid = call(
        functools.partial(out_oth_body, n),
        (share, shape((rows, part), F32)),
        (partner(own), w_near, total, triples[3]),
        [VM] * 4,
        FLOPS["out"],
        2,
    )

    def hidden_of(sent, gain, gate, up):
        own = exchange(sent)
        return call(
            hidden_body,
            shape((rows, gate.shape[1])),
            (own, partner(own), gain[None], in_vmem(gate), in_vmem(up)),
            [VM] * 5,
            FLOPS["hidden"],
            4,
            [pltpu.VMEM((rows, width), BF16)],
        )

    hidden = hidden_of(after_send, gain_first, gate_first, up_first)
    near = in_vmem(down_first)
    send, keep = [
        call(functools.partial(down_body, other), share, (hidden, near), [VM] * 2, FLOPS["down"], 2)
        for other in (1, 0)
    ]
    summed = call(add_body, share, (keep, partner(send)), [VM] * 2, FLOPS["add"], 2)
    first_send, resid = call(
        settle_body, (share, shape((rows, part), F32)), (exchange(summed), resid), [VM] * 2, FLOPS["settle"], 2
    )
    hidden = hidden_of(first_send, gain_second, gate_second, up_second)
    blocks = shape((chips, rm, width))
    keep, send = call(last_body, (blocks, blocks), (hidden, in_vmem(down_second), resid), [VM] * 3, 1e9, 4)
    summed = call(add_body, blocks, (keep, partner(send)), [VM] * 2, 1e9, 2)
    out = call(final_body, shape((rm, width)), (exchange(summed),), [VM], 1e9, 2)
    return out.reshape(rows_here, micro, width)


def pick(mesh):
    n = mesh.shape["tensor"]
    if n % 2 == 0 and H % n == 0 and math.gcd(n, 3) == 1:
        return functools.partial(fast_local, n)
    return local


def solution(mesh):
    return jax.shard_map(
        pick(mesh),
        mesh=mesh,
        in_specs=(
            P("tensor", "groups"),
            P("groups"),
            P(),
            P(),
            P(None, "tensor"),
            P(None, "tensor"),
            P(),
            P(None, "tensor"),
            P(None, "tensor"),
            P("tensor", None),
            P(),
            P(None, "tensor"),
            P(None, "tensor"),
            P("tensor", None),
        ),
        out_specs=P("tensor", "groups", None),
        check_vma=False,
    )
```

```python
import functools
import math

import jax
import jax.numpy as jnp
from jax import lax
from jax.experimental import pallas as pl
from jax.experimental.pallas import tpu as pltpu
from jax.sharding import PartitionSpec as P

H = 48
HD = 128
F32 = jnp.float32
BF16 = jnp.bfloat16
VM = pl.BlockSpec(memory_space=pltpu.VMEM)
SM = pl.BlockSpec(memory_space=pltpu.SMEM)
HB = pl.BlockSpec(memory_space=pltpu.HBM)


def norm_rows(values, gain_vec):
    row_mean = jnp.mean(values, axis=-1, keepdims=True)
    centred = values - row_mean
    row_var = jnp.mean(centred * centred, axis=-1, keepdims=True)
    return (centred * lax.rsqrt(row_var + 1e-05) * gain_vec).astype(jnp.bfloat16)


def local_hidden(normed, gate_mat, up_mat):
    gated = jnp.einsum("pmd,dc->pmc", normed, gate_mat, preferred_element_type=jnp.float32)
    lifted = jnp.einsum("pmd,dc->pmc", normed, up_mat, preferred_element_type=jnp.float32)
    return (jax.nn.silu(gated) * lifted).astype(jnp.bfloat16)


def spread_rows(local_rows, row_fn):
    return row_fn(lax.all_gather(local_rows, "tensor", axis=0, tiled=True), jnp.int32(0))


def to_tokens(columns):
    return lax.all_to_all(columns, "tensor", split_axis=0, concat_axis=2, tiled=True)


def down_sum(hidden_all, down_mat):
    return lax.psum_scatter(
        jnp.einsum("pmc,cd->pmd", hidden_all, down_mat, preferred_element_type=jnp.float32),
        "tensor",
        scatter_dimension=0,
        tiled=True,
    )


def local(
    token_ids,
    lengths,
    embed_table,
    gain_attn,
    w_qkv,
    w_out,
    gain_first,
    gate_first,
    up_first,
    down_first,
    gain_second,
    gate_second,
    up_second,
    down_second,
):
    rows_here = token_ids.shape[0]
    micro_count = token_ids.shape[1]
    vocab_size = embed_table.shape[0]
    own_start = lax.axis_index("tensor") * rows_here
    onehot = (token_ids[:, :, None] == jnp.arange(vocab_size)[None, None, :]).astype(jnp.bfloat16)
    embedded = jnp.einsum("pmv,vd->pmd", onehot, embed_table, preferred_element_type=jnp.float32)
    normed_attn = norm_rows(embedded, gain_attn)

    def qkv_rows(row_piece, row_start):
        return jnp.einsum(
            "pmd,dc->pmc", row_piece, w_qkv, preferred_element_type=jnp.float32
        ).astype(jnp.bfloat16)

    projected = to_tokens(spread_rows(normed_attn, qkv_rows))
    feat_width = projected.shape[2] // 3
    queries = projected[..., :feat_width].reshape(rows_here, micro_count, H, HD)
    key_rows = projected[..., feat_width : 2 * feat_width]
    value_rows = projected[..., 2 * feat_width :]
    score_scale = HD ** (-0.5)
    key_piece = lax.all_gather(key_rows, "tensor", axis=0, tiled=True)
    value_piece = lax.all_gather(value_rows, "tensor", axis=0, tiled=True)
    piece_rows = key_piece.shape[0]
    key_heads = key_piece.reshape(piece_rows, micro_count, H, HD)
    value_heads = value_piece.reshape(piece_rows, micro_count, H, HD)
    scores = (
        jnp.einsum("pmhe,qmhe->pmhq", queries, key_heads, preferred_element_type=jnp.float32)
        * score_scale
    )
    positions = jnp.arange(piece_rows)
    live_keys = (positions[None, :] < lengths[:, None]).astype(jnp.float32)
    weights = jnp.exp(scores) * live_keys[None, :, None, :]
    denominator = jnp.sum(weights, axis=-1)
    numerator = jnp.einsum(
        "pmhq,qmhe->pmhe",
        weights.astype(jnp.bfloat16),
        value_heads,
        preferred_element_type=jnp.float32,
    )
    numerator, denominator = (numerator, denominator)
    attended = (
        (numerator / denominator[..., None])
        .reshape(rows_here, micro_count, feat_width)
        .astype(jnp.bfloat16)
    )

    def out_rows(row_piece, row_start):
        return jnp.einsum(
            "pmd,dc->pmc", row_piece, w_out, preferred_element_type=jnp.float32
        ).astype(jnp.bfloat16)

    after_attn = embedded + to_tokens(spread_rows(attended, out_rows)).astype(jnp.float32)

    def first_rows(row_piece, row_start):
        return local_hidden(row_piece, gate_first, up_first)

    hidden_first = spread_rows(norm_rows(after_attn, gain_first), first_rows)
    partial_all = jnp.einsum(
        "pmc,cd->pmd", hidden_first, down_first, preferred_element_type=jnp.float32
    )
    own_rows = lax.dynamic_slice_in_dim(partial_all, own_start, rows_here, 0) + after_attn
    partial_all = lax.dynamic_update_slice_in_dim(partial_all, own_rows, own_start, 0)
    first_all = lax.psum(partial_all, "tensor")
    after_first = lax.dynamic_slice_in_dim(first_all, own_start, rows_here, 0)
    hidden_second = local_hidden(norm_rows(first_all, gain_second), gate_second, up_second)
    after_second = after_first + down_sum(hidden_second, down_second)
    return after_second.astype(jnp.bfloat16)


def dot(a, b):
    return jnp.dot(a, b, preferred_element_type=F32)


def in_vmem(x):
    return pltpu.with_memory_space_constraint(x, pltpu.VMEM)


def call(body, out_shape, args, specs, flops, limit_mib, scratch=()):
    many = isinstance(out_shape, (tuple, list))
    return pl.pallas_call(
        body,
        out_shape=out_shape,
        in_specs=specs,
        out_specs=[VM] * len(out_shape) if many else VM,
        scratch_shapes=list(scratch),
        compiler_params=pltpu.CompilerParams(vmem_limit_bytes=limit_mib << 20),
        cost_estimate=pl.CostEstimate(flops=int(flops), transcendentals=0, bytes_accessed=1 << 20),
    )(*args)


def project_body(
    pieces, ahead, ids_hbm, table_hbm, gain_hbm, w_hbm, t0_ref, t1_ref, t2_ref, cols_ref, hot_ref,
    ids_ref, table, gain, w_buf, normed, sems, w_sems,
):
    me = lax.axis_index("tensor")
    depth = w_hbm.shape[0] // pieces
    small = [
        pltpu.make_async_copy(table_hbm, table, sems.at[0]),
        pltpu.make_async_copy(gain_hbm, gain, sems.at[1]),
    ]
    ids = pltpu.make_async_copy(ids_hbm, ids_ref, sems.at[2])
    ids.start()
    copies = [
        pltpu.make_async_copy(
            w_hbm.at[pl.ds(i * depth, depth)], w_buf.at[pl.ds(i * depth, depth)], w_sems.at[i]
        )
        for i in range(pieces)
    ]
    for one in small + copies[:2]:
        one.start()
    ids.wait()
    chips, height, lanes = hot_ref.shape
    rows_here, micro = ids_ref.shape
    row_at = lax.broadcasted_iota(jnp.int32, (height, lanes), 0)
    word_at = lax.broadcasted_iota(jnp.int32, (height, lanes), 1)
    hot = jnp.zeros((height, lanes), F32)
    for p in range(rows_here):
        for m in range(micro):
            here = (row_at == p * micro + m) & (word_at == ids_ref[p, m])
            hot = jnp.where(here, 1.0, hot)
    for i in range(chips):
        hot_ref[i] = hot
    for one in small:
        one.wait()
    for one in copies[2:ahead]:
        one.start()
    values = table[...].astype(F32)
    centred = values - jnp.mean(values, axis=-1, keepdims=True)
    var = jnp.mean(centred * centred, axis=-1, keepdims=True)
    normed[...] = (centred * lax.rsqrt(var + 1e-05) * gain[...]).astype(BF16)
    width = cols_ref.shape[1]
    cols_ref[...] = table[:, pl.ds(pl.multiple_of(me * width, 128), width)]
    total = jnp.zeros((normed.shape[0], w_hbm.shape[1]), F32)
    for i, one in enumerate(copies):
        one.wait()
        if i + ahead < pieces:
            copies[i + ahead].start()
        total += dot(normed[:, i * depth : (i + 1) * depth], w_buf[i * depth : (i + 1) * depth, :])
    for i, ref in enumerate((t0_ref, t1_ref, t2_ref)):
        ref[...] = total[:, i * width : (i + 1) * width].astype(BF16)


def owned(n, d):
    return lax.rem(3 * d + 1, n)


def attend_body(n, micro, rm, lens_ref, hot_ref, t0_ref, t1_ref, t2_ref, cols_ref, out_ref, emb_ref):
    head = owned(n, lax.axis_index("tensor"))
    vocab = cols_ref.shape[0]
    onehot = jnp.concatenate([hot_ref[p, :rm, :vocab] for p in range(hot_ref.shape[0])], axis=0).astype(BF16)
    emb_ref[...] = dot(onehot, cols_ref[...])
    got = [dot(onehot, ref[...]).astype(BF16) for ref in (t0_ref, t1_ref, t2_ref)]

    def block(b):
        at = lax.rem(head + b * n, 3)
        return jnp.where(at == 0, got[0], jnp.where(at == 1, got[1], got[2]))

    queries, keys, values = block(0), block(1), block(2)
    rows, width = queries.shape
    row_at = lax.broadcasted_iota(jnp.int32, (rows, rows), 0)
    key_at = lax.broadcasted_iota(jnp.int32, (rows, rows), 1)
    live = jnp.zeros((rows, rows), jnp.bool_)
    for m in range(micro):
        both = (row_at % micro == m) & (key_at % micro == m)
        live = live | (both & (key_at // micro < lens_ref[m]))
    for h in range(width // HD):
        cols = slice(h * HD, (h + 1) * HD)
        scores = lax.dot_general(
            queries[:, cols], keys[:, cols], (((1,), (1,)), ((), ())), preferred_element_type=F32
        ) * (HD ** (-0.5))
        weights = jnp.where(live, jnp.exp(scores), 0.0)
        denominator = jnp.sum(weights, axis=-1, keepdims=True)
        numerator = dot(weights.astype(BF16), values[:, cols])
        attended = (numerator / denominator).astype(BF16)
        for e in range(out_ref.shape[0]):
            out_ref[e, :, cols] = attended


def out_sum(n, ref, c, w_ref):
    chips, rows, width = ref.shape
    total = jnp.zeros((rows, width), F32)
    for e in range(chips):
        at = pl.multiple_of(owned(n, 2 * e + c) * width, 128)
        total += dot(ref[e], w_ref[pl.ds(at, width), :])
    return total


def out_own_body(n, own_ref, w_ref, total_ref):
    core = lax.rem(lax.axis_index("tensor"), 2)
    total_ref[...] = out_sum(n, own_ref, core, w_ref)


def out_oth_body(n, oth_ref, w_ref, total_ref, emb_ref, send_ref, resid_ref):
    core = lax.rem(lax.axis_index("tensor"), 2)
    total = total_ref[...] + out_sum(n, oth_ref, 1 - core, w_ref)
    after = emb_ref[...] + total.astype(BF16).astype(F32)
    resid_ref[...] = after
    for e in range(send_ref.shape[0]):
        send_ref[e] = after.astype(BF16)


def hidden_body(own_ref, oth_ref, gain_ref, g_ref, u_ref, h_ref, normed):
    core = lax.rem(lax.axis_index("tensor"), 2)
    chips, rows, width = own_ref.shape
    own, oth = own_ref[...].astype(F32), oth_ref[...].astype(F32)
    count = 2 * chips * width

    def row_sum(a, b):
        return jnp.sum(jnp.sum(a + b, axis=0), axis=-1, keepdims=True)

    mean = row_sum(own, oth) / count
    own, oth = own - mean[None], oth - mean[None]
    scale = lax.rsqrt(row_sum(own * own, oth * oth) / count + 1e-05)
    for e in range(chips):
        for x, c in ((own, core), (oth, 1 - core)):
            at = pl.ds(pl.multiple_of((2 * e + c) * width, 128), width)
            normed[:, at] = (x[e] * scale * gain_ref[:, at]).astype(BF16)
    step = 256
    for j in range(0, g_ref.shape[1], step):
        gated = dot(normed[...], g_ref[:, j : j + step])
        lifted = dot(normed[...], u_ref[:, j : j + step])
        h_ref[:, j : j + step] = (jax.nn.silu(gated) * lifted).astype(BF16)


def down_body(other, h_ref, d_ref, out_ref):
    core = lax.rem(lax.axis_index("tensor") + other, 2)
    chips, rows, width = out_ref.shape
    for e in range(chips):
        at = pl.multiple_of((2 * e + core) * width, 128)
        out_ref[e] = dot(h_ref[...], d_ref[:, pl.ds(at, width)]).astype(BF16)


def add_body(a_ref, b_ref, out_ref):
    out_ref[...] = (a_ref[...].astype(F32) + b_ref[...].astype(F32)).astype(BF16)


def settle_body(got_ref, resid_ref, send_ref, after_ref):
    after = resid_ref[...] + jnp.sum(got_ref[...].astype(F32), axis=0)
    after_ref[...] = after
    for e in range(send_ref.shape[0]):
        send_ref[e] = after.astype(BF16)


def last_body(h_ref, d_ref, resid_ref, keep_ref, send_ref):
    me = lax.axis_index("tensor")
    core = lax.rem(me, 2)
    chips, rm, _ = keep_ref.shape
    rows, width = resid_ref.shape
    half = rows // 2
    to = lax.broadcasted_iota(jnp.int32, (rows, rows), 0)
    at = lax.broadcasted_iota(jnp.int32, (rows, rows), 1)
    rest = to % half
    side = jnp.where(to < half, core, 1 - core)
    moved = at == (2 * (rest // rm) + side) * rm + rest % rm
    hidden = dot(moved.astype(BF16), h_ref[...]).astype(BF16)
    resid = jnp.dot(
        moved.astype(F32), resid_ref[...], precision=lax.Precision.HIGHEST, preferred_element_type=F32
    )
    for k in range(d_ref.shape[1] // width):
        cols = slice(k * width, (k + 1) * width)
        part = dot(hidden, d_ref[:, cols]) + jnp.where(me == k, resid, 0.0)
        for e in range(chips):
            keep_ref[e, :, cols] = part[e * rm : (e + 1) * rm].astype(BF16)
            send_ref[e, :, cols] = part[half + e * rm : half + (e + 1) * rm].astype(BF16)


def final_body(got_ref, out_ref):
    out_ref[...] = jnp.sum(got_ref[...].astype(F32), axis=0).astype(BF16)


FLOPS = {
    "project": 5e10,
    "attend": 1e10,
    "out": 3e9,
    "hidden": 5e9,
    "down": 5e10,
    "add": 5e10,
    "settle": 5e10,
}


def fast_local(
    n,
    token_ids,
    lengths,
    embed_table,
    gain_attn,
    w_qkv,
    w_out,
    gain_first,
    gate_first,
    up_first,
    down_first,
    gain_second,
    gate_second,
    up_second,
    down_second,
):
    rows_here, micro = token_ids.shape
    rows = n * rows_here * micro
    vocab, width = embed_table.shape
    chips = n // 2
    part = width // n
    same_core = [[2 * e + c for e in range(chips)] for c in range(2)]

    def exchange(x):
        return lax.all_to_all(x, "tensor", 0, 0, tiled=True, axis_index_groups=same_core)

    def partner(x):
        return lax.ppermute(x, "tensor", [(i, i ^ 1) for i in range(n)])

    def shape(dims, dtype=BF16):
        return jax.ShapeDtypeStruct(dims, dtype)

    rm = rows_here * micro
    pieces, ahead = 12, 5
    far = [pltpu.with_memory_space_constraint(x, pltpu.HBM) for x in (token_ids, embed_table, gain_attn[None], w_qkv)]
    triple = shape((vocab, part))
    t0, t1, t2, cols, marks = call(
        functools.partial(project_body, pieces, ahead),
        [triple] * 4 + [shape((n, -(-rm // 8) * 8, -(-vocab // 128) * 128), F32)],
        far,
        [HB] * 4,
        FLOPS["project"],
        24,
        [
            pltpu.SMEM(token_ids.shape, jnp.int32),
            pltpu.VMEM(embed_table.shape, BF16),
            pltpu.VMEM((1, width), F32),
            pltpu.VMEM(w_qkv.shape, BF16),
            pltpu.VMEM((vocab, width), BF16),
            pltpu.SemaphoreType.DMA((3,)),
            pltpu.SemaphoreType.DMA((pieces,)),
        ],
    )
    turn = pow(3, -1, n)
    t0 = lax.ppermute(t0, "tensor", [(d, (d - turn) % n) for d in range(n)])
    t2 = lax.ppermute(t2, "tensor", [(d, (d + turn) % n) for d in range(n)])
    hot = lax.all_to_all(marks, "tensor", 0, 0, tiled=True)
    share = shape((chips, rows, part))
    attended, embedded = call(
        functools.partial(attend_body, n, micro, rm),
        (share, shape((rows, part), F32)),
        (lengths, hot, t0, t1, t2, cols),
        [SM] + [VM] * 5,
        FLOPS["attend"],
        2,
    )
    own = exchange(attended)
    w_near = in_vmem(w_out)
    total = call(
        functools.partial(out_own_body, n), shape((rows, part), F32), (own, w_near), [VM] * 2, FLOPS["out"], 2
    )
    after_send, resid = call(
        functools.partial(out_oth_body, n),
        (share, shape((rows, part), F32)),
        (partner(own), w_near, total, embedded),
        [VM] * 4,
        FLOPS["out"],
        2,
    )

    def hidden_of(sent, gain, gate, up):
        own = exchange(sent)
        return call(
            hidden_body,
            shape((rows, gate.shape[1])),
            (own, partner(own), gain[None], in_vmem(gate), in_vmem(up)),
            [VM] * 5,
            FLOPS["hidden"],
            4,
            [pltpu.VMEM((rows, width), BF16)],
        )

    hidden = hidden_of(after_send, gain_first, gate_first, up_first)
    near = in_vmem(down_first)
    send, keep = [
        call(functools.partial(down_body, other), share, (hidden, near), [VM] * 2, FLOPS["down"], 2)
        for other in (1, 0)
    ]
    summed = call(add_body, share, (keep, partner(send)), [VM] * 2, FLOPS["add"], 2)
    first_send, resid = call(
        settle_body, (share, shape((rows, part), F32)), (exchange(summed), resid), [VM] * 2, FLOPS["settle"], 2
    )
    hidden = hidden_of(first_send, gain_second, gate_second, up_second)
    blocks = shape((chips, rm, width))
    keep, send = call(last_body, (blocks, blocks), (hidden, in_vmem(down_second), resid), [VM] * 3, 1e9, 4)
    summed = call(add_body, blocks, (keep, partner(send)), [VM] * 2, 1e9, 2)
    out = call(final_body, shape((rm, width)), (exchange(summed),), [VM], 1e9, 2)
    return out.reshape(rows_here, micro, width)


def pick(mesh):
    n = mesh.shape["tensor"]
    if n % 2 == 0 and H % n == 0 and math.gcd(n, 3) == 1:
        return functools.partial(fast_local, n)
    return local


def solution(mesh):
    return jax.shard_map(
        pick(mesh),
        mesh=mesh,
        in_specs=(
            P("tensor", "groups"),
            P("groups"),
            P(),
            P(),
            P(None, "tensor"),
            P(None, "tensor"),
            P(),
            P(None, "tensor"),
            P(None, "tensor"),
            P("tensor", None),
            P(),
            P(None, "tensor"),
            P(None, "tensor"),
            P("tensor", None),
        ),
        out_specs=P("tensor", "groups", None),
        check_vma=False,
    )
```

```python
import functools
import math

import jax
import jax.numpy as jnp
from jax import lax
from jax.experimental import pallas as pl
from jax.experimental.pallas import tpu as pltpu
from jax.sharding import PartitionSpec as P

H = 48
HD = 128
F32 = jnp.float32
BF16 = jnp.bfloat16
VM = pl.BlockSpec(memory_space=pltpu.VMEM)
SM = pl.BlockSpec(memory_space=pltpu.SMEM)
HB = pl.BlockSpec(memory_space=pltpu.HBM)


def norm_rows(values, gain_vec):
    row_mean = jnp.mean(values, axis=-1, keepdims=True)
    centred = values - row_mean
    row_var = jnp.mean(centred * centred, axis=-1, keepdims=True)
    return (centred * lax.rsqrt(row_var + 1e-05) * gain_vec).astype(jnp.bfloat16)


def local_hidden(normed, gate_mat, up_mat):
    gated = jnp.einsum("pmd,dc->pmc", normed, gate_mat, preferred_element_type=jnp.float32)
    lifted = jnp.einsum("pmd,dc->pmc", normed, up_mat, preferred_element_type=jnp.float32)
    return (jax.nn.silu(gated) * lifted).astype(jnp.bfloat16)


def spread_rows(local_rows, row_fn):
    return row_fn(lax.all_gather(local_rows, "tensor", axis=0, tiled=True), jnp.int32(0))


def to_tokens(columns):
    return lax.all_to_all(columns, "tensor", split_axis=0, concat_axis=2, tiled=True)


def down_sum(hidden_all, down_mat):
    return lax.psum_scatter(
        jnp.einsum("pmc,cd->pmd", hidden_all, down_mat, preferred_element_type=jnp.float32),
        "tensor",
        scatter_dimension=0,
        tiled=True,
    )


def local(
    token_ids,
    lengths,
    embed_table,
    gain_attn,
    w_qkv,
    w_out,
    gain_first,
    gate_first,
    up_first,
    down_first,
    gain_second,
    gate_second,
    up_second,
    down_second,
):
    rows_here = token_ids.shape[0]
    micro_count = token_ids.shape[1]
    vocab_size = embed_table.shape[0]
    own_start = lax.axis_index("tensor") * rows_here
    onehot = (token_ids[:, :, None] == jnp.arange(vocab_size)[None, None, :]).astype(jnp.bfloat16)
    embedded = jnp.einsum("pmv,vd->pmd", onehot, embed_table, preferred_element_type=jnp.float32)
    normed_attn = norm_rows(embedded, gain_attn)

    def qkv_rows(row_piece, row_start):
        return jnp.einsum(
            "pmd,dc->pmc", row_piece, w_qkv, preferred_element_type=jnp.float32
        ).astype(jnp.bfloat16)

    projected = to_tokens(spread_rows(normed_attn, qkv_rows))
    feat_width = projected.shape[2] // 3
    queries = projected[..., :feat_width].reshape(rows_here, micro_count, H, HD)
    key_rows = projected[..., feat_width : 2 * feat_width]
    value_rows = projected[..., 2 * feat_width :]
    score_scale = HD ** (-0.5)
    key_piece = lax.all_gather(key_rows, "tensor", axis=0, tiled=True)
    value_piece = lax.all_gather(value_rows, "tensor", axis=0, tiled=True)
    piece_rows = key_piece.shape[0]
    key_heads = key_piece.reshape(piece_rows, micro_count, H, HD)
    value_heads = value_piece.reshape(piece_rows, micro_count, H, HD)
    scores = (
        jnp.einsum("pmhe,qmhe->pmhq", queries, key_heads, preferred_element_type=jnp.float32)
        * score_scale
    )
    positions = jnp.arange(piece_rows)
    live_keys = (positions[None, :] < lengths[:, None]).astype(jnp.float32)
    weights = jnp.exp(scores) * live_keys[None, :, None, :]
    denominator = jnp.sum(weights, axis=-1)
    numerator = jnp.einsum(
        "pmhq,qmhe->pmhe",
        weights.astype(jnp.bfloat16),
        value_heads,
        preferred_element_type=jnp.float32,
    )
    numerator, denominator = (numerator, denominator)
    attended = (
        (numerator / denominator[..., None])
        .reshape(rows_here, micro_count, feat_width)
        .astype(jnp.bfloat16)
    )

    def out_rows(row_piece, row_start):
        return jnp.einsum(
            "pmd,dc->pmc", row_piece, w_out, preferred_element_type=jnp.float32
        ).astype(jnp.bfloat16)

    after_attn = embedded + to_tokens(spread_rows(attended, out_rows)).astype(jnp.float32)

    def first_rows(row_piece, row_start):
        return local_hidden(row_piece, gate_first, up_first)

    hidden_first = spread_rows(norm_rows(after_attn, gain_first), first_rows)
    partial_all = jnp.einsum(
        "pmc,cd->pmd", hidden_first, down_first, preferred_element_type=jnp.float32
    )
    own_rows = lax.dynamic_slice_in_dim(partial_all, own_start, rows_here, 0) + after_attn
    partial_all = lax.dynamic_update_slice_in_dim(partial_all, own_rows, own_start, 0)
    first_all = lax.psum(partial_all, "tensor")
    after_first = lax.dynamic_slice_in_dim(first_all, own_start, rows_here, 0)
    hidden_second = local_hidden(norm_rows(first_all, gain_second), gate_second, up_second)
    after_second = after_first + down_sum(hidden_second, down_second)
    return after_second.astype(jnp.bfloat16)


def dot(a, b):
    return jnp.dot(a, b, preferred_element_type=F32)


def in_vmem(x):
    return pltpu.with_memory_space_constraint(x, pltpu.VMEM)


def call(body, out_shape, args, specs, flops, limit_mib, scratch=()):
    many = isinstance(out_shape, (tuple, list))
    return pl.pallas_call(
        body,
        out_shape=out_shape,
        in_specs=specs,
        out_specs=[VM] * len(out_shape) if many else VM,
        scratch_shapes=list(scratch),
        compiler_params=pltpu.CompilerParams(vmem_limit_bytes=limit_mib << 20),
        cost_estimate=pl.CostEstimate(flops=int(flops), transcendentals=0, bytes_accessed=1 << 20),
    )(*args)


def project_body(
    pieces, ahead, ids_hbm, table_hbm, gain_hbm, w_hbm, t0_ref, t1_ref, t2_ref, cols_ref, hot_ref,
    ids_ref, table, gain, w_buf, normed, sems, w_sems,
):
    me = lax.axis_index("tensor")
    depth = w_hbm.shape[0] // pieces
    small = [
        pltpu.make_async_copy(table_hbm, table, sems.at[0]),
        pltpu.make_async_copy(gain_hbm, gain, sems.at[1]),
    ]
    ids = pltpu.make_async_copy(ids_hbm, ids_ref, sems.at[2])
    ids.start()
    copies = [
        pltpu.make_async_copy(
            w_hbm.at[pl.ds(i * depth, depth)], w_buf.at[pl.ds(i * depth, depth)], w_sems.at[i]
        )
        for i in range(pieces)
    ]
    for one in small + copies[:2]:
        one.start()
    ids.wait()
    chips, height, lanes = hot_ref.shape
    rows_here, micro = ids_ref.shape
    row_at = lax.broadcasted_iota(jnp.int32, (height, lanes), 0)
    word_at = lax.broadcasted_iota(jnp.int32, (height, lanes), 1)
    hot = jnp.zeros((height, lanes), F32)
    for p in range(rows_here):
        for m in range(micro):
            here = (row_at == p * micro + m) & (word_at == ids_ref[p, m])
            hot = jnp.where(here, 1.0, hot)
    for i in range(chips):
        hot_ref[i] = hot
    for one in small:
        one.wait()
    for one in copies[2:ahead]:
        one.start()
    values = table[...].astype(F32)
    centred = values - jnp.mean(values, axis=-1, keepdims=True)
    var = jnp.mean(centred * centred, axis=-1, keepdims=True)
    normed[...] = (centred * lax.rsqrt(var + 1e-05) * gain[...]).astype(BF16)
    width = cols_ref.shape[1]
    cols_ref[...] = table[:, pl.ds(pl.multiple_of(me * width, 128), width)]
    total = jnp.zeros((normed.shape[0], w_hbm.shape[1]), F32)
    for i, one in enumerate(copies):
        one.wait()
        if i + ahead < pieces:
            copies[i + ahead].start()
        total += dot(normed[:, i * depth : (i + 1) * depth], w_buf[i * depth : (i + 1) * depth, :])
    for i, ref in enumerate((t0_ref, t1_ref, t2_ref)):
        ref[...] = total[:, i * width : (i + 1) * width].astype(BF16)


def owned(n, d):
    return lax.rem(3 * d + 1, n)


def attend_body(n, micro, rm, lens_ref, hot_ref, t0_ref, t1_ref, t2_ref, cols_ref, out_ref, emb_ref):
    head = owned(n, lax.axis_index("tensor"))
    vocab = cols_ref.shape[0]
    onehot = jnp.concatenate([hot_ref[p, :rm, :vocab] for p in range(hot_ref.shape[0])], axis=0).astype(BF16)
    emb_ref[...] = dot(onehot, cols_ref[...])
    got = [dot(onehot, ref[...]).astype(BF16) for ref in (t0_ref, t1_ref, t2_ref)]

    def block(b):
        at = lax.rem(head + b * n, 3)
        return jnp.where(at == 0, got[0], jnp.where(at == 1, got[1], got[2]))

    queries, keys, values = block(0), block(1), block(2)
    rows, width = queries.shape
    row_at = lax.broadcasted_iota(jnp.int32, (rows, rows), 0)
    key_at = lax.broadcasted_iota(jnp.int32, (rows, rows), 1)
    live = jnp.zeros((rows, rows), jnp.bool_)
    for m in range(micro):
        both = (row_at % micro == m) & (key_at % micro == m)
        live = live | (both & (key_at // micro < lens_ref[m]))
    for h in range(width // HD):
        cols = slice(h * HD, (h + 1) * HD)
        scores = lax.dot_general(
            queries[:, cols], keys[:, cols], (((1,), (1,)), ((), ())), preferred_element_type=F32
        ) * (HD ** (-0.5))
        weights = jnp.where(live, jnp.exp(scores), 0.0)
        denominator = jnp.sum(weights, axis=-1, keepdims=True)
        numerator = dot(weights.astype(BF16), values[:, cols])
        attended = (numerator / denominator).astype(BF16)
        for e in range(out_ref.shape[0]):
            out_ref[e, :, cols] = attended


def out_sum(n, ref, c, w_ref):
    chips, rows, width = ref.shape
    total = jnp.zeros((rows, width), F32)
    for e in range(chips):
        at = pl.multiple_of(owned(n, 2 * e + c) * width, 128)
        total += dot(ref[e], w_ref[pl.ds(at, width), :])
    return total


def out_own_body(n, own_ref, w_ref, total_ref):
    core = lax.rem(lax.axis_index("tensor"), 2)
    total_ref[...] = out_sum(n, own_ref, core, w_ref)


def out_oth_body(n, oth_ref, w_ref, total_ref, emb_ref, send_ref, resid_ref):
    core = lax.rem(lax.axis_index("tensor"), 2)
    total = total_ref[...] + out_sum(n, oth_ref, 1 - core, w_ref)
    after = emb_ref[...] + total.astype(BF16).astype(F32)
    resid_ref[...] = after
    for e in range(send_ref.shape[0]):
        send_ref[e] = after.astype(BF16)


def join_body(*refs):
    for i, ref in enumerate(refs[:-1]):
        refs[-1][i] = ref[0]


def shifted(ref, i, shift, gain_ref, at, y, put):
    rows, width = ref.shape[1:]
    off = ref[i].astype(F32) - shift
    gain = gain_ref[:, pl.ds(at, width)]
    y[:rows, put] = (off * gain).astype(BF16)
    y[rows:, put] = jnp.broadcast_to(gain, (y.shape[0] - rows, width)).astype(BF16)
    return off


def wide(column):
    return jnp.broadcast_to(column, (column.shape[0], 128))


def near_body(own_ref, prt_ref, gain_ref, g_ref, u_ref, *rest):
    ag_ref, au_ref, stat_ref, y = rest[-4:]
    me = lax.axis_index("tensor")
    core = lax.rem(me, 2)
    blocks, rows, width = own_ref.shape
    total = jnp.zeros((rows, width), F32)
    for i in range(blocks):
        total += own_ref[i].astype(F32) + prt_ref[i].astype(F32)
    shift = jnp.sum(total, axis=-1, keepdims=True) / (2 * blocks * width)
    square = jnp.zeros((rows, width), F32)
    for i in range(blocks):
        for ref, c in ((own_ref, core), (prt_ref, 1 - core)):
            at = pl.multiple_of(((me ^ (4 * i)) - core + c) * width, 128)
            put = pl.ds(pl.multiple_of((2 * i + c) * width, 128), width)
            off = shifted(ref, i, shift, gain_ref, at, y, put)
            square += off * off
    stat_ref[0] = wide(shift)
    stat_ref[1] = jnp.zeros_like(stat_ref[1])
    stat_ref[2] = wide(jnp.sum(square, axis=-1, keepdims=True))
    step = g_ref.shape[1] // 2
    for w_ref, out_ref in ((g_ref, ag_ref), (u_ref, au_ref)):
        for j in range(0, g_ref.shape[1], step):
            part = jnp.zeros((y.shape[0], step), F32)
            for i in range(blocks):
                at = pl.multiple_of(((me ^ (4 * i)) - core) * width, 128)
                part += dot(
                    y[:, 2 * i * width : 2 * (i + 1) * width], w_ref[pl.ds(at, 2 * width), j : j + step]
                )
            out_ref[:, j : j + step] = part


def far_body(flip, last, got_ref, gain_ref, g_ref, u_ref, ag_ref, au_ref, stat_ref, *rest):
    me = lax.axis_index("tensor") ^ flip
    rest = rest[-2 if last else -4 :]
    y = rest[-1]
    blocks, rows, width = got_ref.shape
    shift = stat_ref[0][:, :1]
    total = jnp.zeros((rows, width), F32)
    square = jnp.zeros((rows, width), F32)
    for i in range(blocks):
        at = pl.multiple_of((me ^ (4 * i)) * width, 128)
        off = shifted(got_ref, i, shift, gain_ref, at, y, slice(i * width, (i + 1) * width))
        total += off
        square += off * off
    first = stat_ref[1] + wide(jnp.sum(total, axis=-1, keepdims=True))
    second = stat_ref[2] + wide(jnp.sum(square, axis=-1, keepdims=True))
    if last:
        count = 4 * blocks * width
        lean = first[:, :1] / count
        scale = lax.rsqrt(jnp.maximum(second[:, :1] / count - lean * lean, 0.0) + 1e-05)
    else:
        rest[2][0], rest[2][1], rest[2][2] = stat_ref[0], first, second
    step = 256
    for j in range(0, g_ref.shape[1], step):
        cols = slice(j, j + step)
        parts = []
        for w_ref, acc_ref in ((g_ref, ag_ref), (u_ref, au_ref)):
            part = acc_ref[:, cols]
            for i in range(blocks):
                at = pl.multiple_of((me ^ (4 * i)) * width, 128)
                part += dot(y[:, i * width : (i + 1) * width], w_ref[pl.ds(at, width), cols])
            parts.append(part)
        if last:
            gated, lifted = [scale * (part[:rows] - lean * part[rows : rows + 1]) for part in parts]
            rest[0][:, cols] = (jax.nn.silu(gated) * lifted).astype(BF16)
        else:
            rest[0][:, cols], rest[1][:, cols] = parts


def down_body(other, h_ref, d_ref, out_ref):
    core = lax.rem(lax.axis_index("tensor") + other, 2)
    chips, rows, width = out_ref.shape
    for e in range(chips):
        at = pl.multiple_of((2 * e + core) * width, 128)
        out_ref[e] = dot(h_ref[...], d_ref[:, pl.ds(at, width)]).astype(BF16)


def add_body(a_ref, b_ref, out_ref):
    out_ref[...] = (a_ref[...].astype(F32) + b_ref[...].astype(F32)).astype(BF16)


def settle_body(got_ref, resid_ref, send_ref, after_ref):
    after = resid_ref[...] + jnp.sum(got_ref[...].astype(F32), axis=0)
    after_ref[...] = after
    for e in range(send_ref.shape[0]):
        send_ref[e] = after.astype(BF16)


def last_body(h_ref, d_ref, resid_ref, keep_ref, send_ref):
    me = lax.axis_index("tensor")
    core = lax.rem(me, 2)
    chips, rm, _ = keep_ref.shape
    rows, width = resid_ref.shape
    half = rows // 2
    to = lax.broadcasted_iota(jnp.int32, (rows, rows), 0)
    at = lax.broadcasted_iota(jnp.int32, (rows, rows), 1)
    rest = to % half
    side = jnp.where(to < half, core, 1 - core)
    moved = at == (2 * (rest // rm) + side) * rm + rest % rm
    hidden = dot(moved.astype(BF16), h_ref[...]).astype(BF16)
    resid = jnp.dot(
        moved.astype(F32), resid_ref[...], precision=lax.Precision.HIGHEST, preferred_element_type=F32
    )
    for k in range(d_ref.shape[1] // width):
        cols = slice(k * width, (k + 1) * width)
        part = dot(hidden, d_ref[:, cols]) + jnp.where(me == k, resid, 0.0)
        for e in range(chips):
            keep_ref[e, :, cols] = part[e * rm : (e + 1) * rm].astype(BF16)
            send_ref[e, :, cols] = part[half + e * rm : half + (e + 1) * rm].astype(BF16)


def final_body(got_ref, out_ref):
    out_ref[...] = jnp.sum(got_ref[...].astype(F32), axis=0).astype(BF16)


HELD = (('near', 'beside', 'across'), ('near', 'beside', 'across'))


FLOPS = {'project': 50000000000.0, 'attend': 20000000000.0, 'out': 3000000000.0, 'join': 1000000000.0, 'near': 1000000000.0, 'far': 500000000.0, 'down': 50000000000.0, 'add': 50000000000.0, 'settle': 50000000000.0}


def fast_local(
    n,
    token_ids,
    lengths,
    embed_table,
    gain_attn,
    w_qkv,
    w_out,
    gain_first,
    gate_first,
    up_first,
    down_first,
    gain_second,
    gate_second,
    up_second,
    down_second,
):
    rows_here, micro = token_ids.shape
    rows = n * rows_here * micro
    vocab, width = embed_table.shape
    chips = n // 2
    part = width // n
    same_core = [[2 * e + c for e in range(chips)] for c in range(2)]

    def exchange(x):
        return lax.all_to_all(x, "tensor", 0, 0, tiled=True, axis_index_groups=same_core)

    def partner(x):
        return lax.ppermute(x, "tensor", [(i, i ^ 1) for i in range(n)])

    def shape(dims, dtype=BF16):
        return jax.ShapeDtypeStruct(dims, dtype)

    rm = rows_here * micro
    pieces, ahead = 12, 5
    far = [pltpu.with_memory_space_constraint(x, pltpu.HBM) for x in (token_ids, embed_table, gain_attn[None], w_qkv)]
    triple = shape((vocab, part))
    t0, t1, t2, cols, marks = call(
        functools.partial(project_body, pieces, ahead),
        [triple] * 4 + [shape((n, -(-rm // 8) * 8, -(-vocab // 128) * 128), F32)],
        far,
        [HB] * 4,
        FLOPS["project"],
        24,
        [
            pltpu.SMEM(token_ids.shape, jnp.int32),
            pltpu.VMEM(embed_table.shape, BF16),
            pltpu.VMEM((1, width), F32),
            pltpu.VMEM(w_qkv.shape, BF16),
            pltpu.VMEM((vocab, width), BF16),
            pltpu.SemaphoreType.DMA((3,)),
            pltpu.SemaphoreType.DMA((pieces,)),
        ],
    )
    turn = pow(3, -1, n)
    t0 = lax.ppermute(t0, "tensor", [(d, (d - turn) % n) for d in range(n)])
    t2 = lax.ppermute(t2, "tensor", [(d, (d + turn) % n) for d in range(n)])
    hot = lax.all_to_all(marks, "tensor", 0, 0, tiled=True)
    share = shape((chips, rows, part))
    attended, embedded = call(
        functools.partial(attend_body, n, micro, rm),
        (share, shape((rows, part), F32)),
        (lengths, hot, t0, t1, t2, cols),
        [SM] + [VM] * 5,
        FLOPS["attend"],
        2,
    )
    own = exchange(attended)
    w_near = in_vmem(w_out)
    total = call(
        functools.partial(out_own_body, n), shape((rows, part), F32), (own, w_near), [VM] * 2, FLOPS["out"], 2
    )
    after_send, resid = call(
        functools.partial(out_oth_body, n),
        (shape((1, rows, part)), shape((rows, part), F32)),
        (partner(own), w_near, total, embedded),
        [VM] * 4,
        FLOPS["out"],
        2,
    )

    def toward(x, flip):
        return lax.ppermute(x, "tensor", [(i, i ^ flip) for i in range(n)])

    def hidden_of(sent, gain, gate, up, down, held):
        keep = [[down] * (name in held) for name in ("near", "beside", "across")]
        blocks, units = n // 4, gate.shape[1]
        gain, gate, up = gain[None], in_vmem(gate), in_vmem(up)
        own = call(
            join_body,
            shape((blocks, rows, part)),
            (sent, *[toward(sent, 4 * i) for i in range(1, blocks)]),
            [VM] * blocks,
            FLOPS["join"],
            2,
        )
        beside = toward(own, 2)
        accs = (shape((rows + 16, units), F32), shape((rows + 16, units), F32), shape((3, rows, 128), F32))
        part_sums = call(
            near_body,
            accs,
            (own, toward(own, 1), gain, gate, up, *keep[0]),
            [VM] * (5 + len(keep[0])),
            FLOPS["near"],
            2,
            [pltpu.VMEM((rows + 16, 2 * blocks * part), BF16)],
        )
        y = [pltpu.VMEM((rows + 16, blocks * part), BF16)]
        beside, *part_sums = lax.optimization_barrier((beside, *part_sums))
        across = toward(beside, 1)
        part_sums = call(
            functools.partial(far_body, 2, False),
            accs,
            (beside, gain, gate, up, *part_sums, *keep[1]),
            [VM] * (7 + len(keep[1])),
            FLOPS["far"],
            1,
            y,
        )
        return call(
            functools.partial(far_body, 3, True),
            shape((rows, units)),
            (across, gain, gate, up, *part_sums, *keep[2]),
            [VM] * (7 + len(keep[2])),
            FLOPS["far"],
            1,
            y,
        )

    near = in_vmem(down_first)
    hidden = hidden_of(after_send, gain_first, gate_first, up_first, near, HELD[0])
    send, keep = [
        call(functools.partial(down_body, other), share, (hidden, near), [VM] * 2, FLOPS["down"], 2)
        for other in (1, 0)
    ]
    summed = call(add_body, share, (keep, partner(send)), [VM] * 2, FLOPS["add"], 2)
    first_send, resid = call(
        settle_body, (shape((1, rows, part)), shape((rows, part), F32)), (exchange(summed), resid), [VM] * 2, FLOPS["settle"], 2
    )
    near = in_vmem(down_second)
    hidden = hidden_of(first_send, gain_second, gate_second, up_second, near, HELD[1])
    blocks = shape((chips, rm, width))
    keep, send = call(last_body, (blocks, blocks), (hidden, near, resid), [VM] * 3, 1e9, 2)
    summed = call(add_body, blocks, (keep, partner(send)), [VM] * 2, 1e9, 2)
    out = call(final_body, shape((rm, width)), (exchange(summed),), [VM], 1e9, 2)
    return out.reshape(rows_here, micro, width)


def pick(mesh):
    n = mesh.shape["tensor"]
    if n % 4 == 0 and H % n == 0 and math.gcd(n, 3) == 1:
        return functools.partial(fast_local, n)
    return local


def solution(mesh):
    return jax.shard_map(
        pick(mesh),
        mesh=mesh,
        in_specs=(
            P("tensor", "groups"),
            P("groups"),
            P(),
            P(),
            P(None, "tensor"),
            P(None, "tensor"),
            P(),
            P(None, "tensor"),
            P(None, "tensor"),
            P("tensor", None),
            P(),
            P(None, "tensor"),
            P(None, "tensor"),
            P("tensor", None),
        ),
        out_specs=P("tensor", "groups", None),
        check_vma=False,
    )
```

```python
import functools
import math

import jax
import jax.numpy as jnp
from jax import lax
from jax.experimental import pallas as pl
from jax.experimental.pallas import tpu as pltpu
from jax.sharding import PartitionSpec as P

H = 48
HD = 128
F32 = jnp.float32
BF16 = jnp.bfloat16
VM = pl.BlockSpec(memory_space=pltpu.VMEM)
SM = pl.BlockSpec(memory_space=pltpu.SMEM)
HB = pl.BlockSpec(memory_space=pltpu.HBM)


def norm_rows(values, gain_vec):
    row_mean = jnp.mean(values, axis=-1, keepdims=True)
    centred = values - row_mean
    row_var = jnp.mean(centred * centred, axis=-1, keepdims=True)
    return (centred * lax.rsqrt(row_var + 1e-05) * gain_vec).astype(jnp.bfloat16)


def local_hidden(normed, gate_mat, up_mat):
    gated = jnp.einsum("pmd,dc->pmc", normed, gate_mat, preferred_element_type=jnp.float32)
    lifted = jnp.einsum("pmd,dc->pmc", normed, up_mat, preferred_element_type=jnp.float32)
    return (jax.nn.silu(gated) * lifted).astype(jnp.bfloat16)


def spread_rows(local_rows, row_fn):
    return row_fn(lax.all_gather(local_rows, "tensor", axis=0, tiled=True), jnp.int32(0))


def to_tokens(columns):
    return lax.all_to_all(columns, "tensor", split_axis=0, concat_axis=2, tiled=True)


def down_sum(hidden_all, down_mat):
    return lax.psum_scatter(
        jnp.einsum("pmc,cd->pmd", hidden_all, down_mat, preferred_element_type=jnp.float32),
        "tensor",
        scatter_dimension=0,
        tiled=True,
    )


def local(
    token_ids,
    lengths,
    embed_table,
    gain_attn,
    w_qkv,
    w_out,
    gain_first,
    gate_first,
    up_first,
    down_first,
    gain_second,
    gate_second,
    up_second,
    down_second,
):
    rows_here = token_ids.shape[0]
    micro_count = token_ids.shape[1]
    vocab_size = embed_table.shape[0]
    own_start = lax.axis_index("tensor") * rows_here
    onehot = (token_ids[:, :, None] == jnp.arange(vocab_size)[None, None, :]).astype(jnp.bfloat16)
    embedded = jnp.einsum("pmv,vd->pmd", onehot, embed_table, preferred_element_type=jnp.float32)
    normed_attn = norm_rows(embedded, gain_attn)

    def qkv_rows(row_piece, row_start):
        return jnp.einsum(
            "pmd,dc->pmc", row_piece, w_qkv, preferred_element_type=jnp.float32
        ).astype(jnp.bfloat16)

    projected = to_tokens(spread_rows(normed_attn, qkv_rows))
    feat_width = projected.shape[2] // 3
    queries = projected[..., :feat_width].reshape(rows_here, micro_count, H, HD)
    key_rows = projected[..., feat_width : 2 * feat_width]
    value_rows = projected[..., 2 * feat_width :]
    score_scale = HD ** (-0.5)
    key_piece = lax.all_gather(key_rows, "tensor", axis=0, tiled=True)
    value_piece = lax.all_gather(value_rows, "tensor", axis=0, tiled=True)
    piece_rows = key_piece.shape[0]
    key_heads = key_piece.reshape(piece_rows, micro_count, H, HD)
    value_heads = value_piece.reshape(piece_rows, micro_count, H, HD)
    scores = (
        jnp.einsum("pmhe,qmhe->pmhq", queries, key_heads, preferred_element_type=jnp.float32)
        * score_scale
    )
    positions = jnp.arange(piece_rows)
    live_keys = (positions[None, :] < lengths[:, None]).astype(jnp.float32)
    weights = jnp.exp(scores) * live_keys[None, :, None, :]
    denominator = jnp.sum(weights, axis=-1)
    numerator = jnp.einsum(
        "pmhq,qmhe->pmhe",
        weights.astype(jnp.bfloat16),
        value_heads,
        preferred_element_type=jnp.float32,
    )
    numerator, denominator = (numerator, denominator)
    attended = (
        (numerator / denominator[..., None])
        .reshape(rows_here, micro_count, feat_width)
        .astype(jnp.bfloat16)
    )

    def out_rows(row_piece, row_start):
        return jnp.einsum(
            "pmd,dc->pmc", row_piece, w_out, preferred_element_type=jnp.float32
        ).astype(jnp.bfloat16)

    after_attn = embedded + to_tokens(spread_rows(attended, out_rows)).astype(jnp.float32)

    def first_rows(row_piece, row_start):
        return local_hidden(row_piece, gate_first, up_first)

    hidden_first = spread_rows(norm_rows(after_attn, gain_first), first_rows)
    partial_all = jnp.einsum(
        "pmc,cd->pmd", hidden_first, down_first, preferred_element_type=jnp.float32
    )
    own_rows = lax.dynamic_slice_in_dim(partial_all, own_start, rows_here, 0) + after_attn
    partial_all = lax.dynamic_update_slice_in_dim(partial_all, own_rows, own_start, 0)
    first_all = lax.psum(partial_all, "tensor")
    after_first = lax.dynamic_slice_in_dim(first_all, own_start, rows_here, 0)
    hidden_second = local_hidden(norm_rows(first_all, gain_second), gate_second, up_second)
    after_second = after_first + down_sum(hidden_second, down_second)
    return after_second.astype(jnp.bfloat16)


def dot(a, b):
    return jnp.dot(a, b, preferred_element_type=F32)


def in_vmem(x):
    return pltpu.with_memory_space_constraint(x, pltpu.VMEM)


def call(body, out_shape, args, specs, flops, limit_mib, scratch=()):
    many = isinstance(out_shape, (tuple, list))
    return pl.pallas_call(
        body,
        out_shape=out_shape,
        in_specs=specs,
        out_specs=[VM] * len(out_shape) if many else VM,
        scratch_shapes=list(scratch),
        compiler_params=pltpu.CompilerParams(vmem_limit_bytes=limit_mib << 20),
        cost_estimate=pl.CostEstimate(flops=int(flops), transcendentals=0, bytes_accessed=1 << 20),
    )(*args)


def project_body(
    pieces, ahead, ids_hbm, table_hbm, gain_hbm, w_hbm, t0_ref, t1_ref, t2_ref, cols_ref, hot_ref,
    ids_ref, table, gain, w_buf, normed, sems, w_sems,
):
    me = lax.axis_index("tensor")
    depth = w_hbm.shape[0] // pieces
    small = [
        pltpu.make_async_copy(table_hbm, table, sems.at[0]),
        pltpu.make_async_copy(gain_hbm, gain, sems.at[1]),
    ]
    ids = pltpu.make_async_copy(ids_hbm, ids_ref, sems.at[2])
    ids.start()
    copies = [
        pltpu.make_async_copy(
            w_hbm.at[pl.ds(i * depth, depth)], w_buf.at[pl.ds(i * depth, depth)], w_sems.at[i]
        )
        for i in range(pieces)
    ]
    for one in small + copies[:2]:
        one.start()
    ids.wait()
    chips, height, lanes = hot_ref.shape
    rows_here, micro = ids_ref.shape
    row_at = lax.broadcasted_iota(jnp.int32, (height, lanes), 0)
    word_at = lax.broadcasted_iota(jnp.int32, (height, lanes), 1)
    hot = jnp.zeros((height, lanes), F32)
    for p in range(rows_here):
        for m in range(micro):
            here = (row_at == p * micro + m) & (word_at == ids_ref[p, m])
            hot = jnp.where(here, 1.0, hot)
    for i in range(chips):
        hot_ref[i] = hot
    for one in small:
        one.wait()
    for one in copies[2:ahead]:
        one.start()
    values = table[...].astype(F32)
    centred = values - jnp.mean(values, axis=-1, keepdims=True)
    var = jnp.mean(centred * centred, axis=-1, keepdims=True)
    normed[...] = (centred * lax.rsqrt(var + 1e-05) * gain[...]).astype(BF16)
    width = cols_ref.shape[1]
    cols_ref[...] = table[:, pl.ds(pl.multiple_of(me * width, 128), width)]
    total = jnp.zeros((normed.shape[0], w_hbm.shape[1]), F32)
    for i, one in enumerate(copies):
        one.wait()
        if i + ahead < pieces:
            copies[i + ahead].start()
        total += dot(normed[:, i * depth : (i + 1) * depth], w_buf[i * depth : (i + 1) * depth, :])
    for i, ref in enumerate((t0_ref, t1_ref, t2_ref)):
        ref[...] = total[:, i * width : (i + 1) * width].astype(BF16)


def owned(n, d):
    return lax.rem(3 * d + 1, n)


def attend_body(n, micro, rm, lens_ref, hot_ref, t0_ref, t1_ref, t2_ref, cols_ref, out_ref, emb_ref):
    head = owned(n, lax.axis_index("tensor"))
    vocab = cols_ref.shape[0]
    onehot = jnp.concatenate([hot_ref[p, :rm, :vocab] for p in range(hot_ref.shape[0])], axis=0).astype(BF16)
    emb_ref[...] = dot(onehot, cols_ref[...])
    got = [dot(onehot, ref[...]).astype(BF16) for ref in (t0_ref, t1_ref, t2_ref)]

    def block(b):
        at = lax.rem(head + b * n, 3)
        return jnp.where(at == 0, got[0], jnp.where(at == 1, got[1], got[2]))

    queries, keys, values = block(0), block(1), block(2)
    rows, width = queries.shape
    row_at = lax.broadcasted_iota(jnp.int32, (rows, rows), 0)
    key_at = lax.broadcasted_iota(jnp.int32, (rows, rows), 1)
    live = jnp.zeros((rows, rows), jnp.bool_)
    for m in range(micro):
        both = (row_at % micro == m) & (key_at % micro == m)
        live = live | (both & (key_at // micro < lens_ref[m]))
    for h in range(width // HD):
        cols = slice(h * HD, (h + 1) * HD)
        scores = lax.dot_general(
            queries[:, cols], keys[:, cols], (((1,), (1,)), ((), ())), preferred_element_type=F32
        ) * (HD ** (-0.5))
        weights = jnp.where(live, jnp.exp(scores), 0.0)
        denominator = jnp.sum(weights, axis=-1, keepdims=True)
        numerator = dot(weights.astype(BF16), values[:, cols])
        attended = (numerator / denominator).astype(BF16)
        for e in range(out_ref.shape[0]):
            out_ref[e, :, cols] = attended


def out_sum(n, flip, ref, w_ref):
    me = lax.axis_index("tensor") ^ flip
    blocks, rows, width = ref.shape
    total = jnp.zeros((rows, width), F32)
    for i in range(blocks):
        at = pl.multiple_of(owned(n, me ^ (4 * i)) * width, 128)
        total += dot(ref[i], w_ref[pl.ds(at, width), :])
    return total


def out_near_body(n, own_ref, prt_ref, w_ref, total_ref):
    total_ref[...] = out_sum(n, 0, own_ref, w_ref) + out_sum(n, 1, prt_ref, w_ref)


def out_mid_body(n, got_ref, w_ref, near_ref, total_ref):
    total_ref[...] = near_ref[...] + out_sum(n, 2, got_ref, w_ref)


def out_far_body(n, got_ref, w_ref, near_ref, emb_ref, send_ref, resid_ref):
    total = near_ref[...] + out_sum(n, 3, got_ref, w_ref)
    after = emb_ref[...] + total.astype(BF16).astype(F32)
    resid_ref[...] = after
    send_ref[0] = after.astype(BF16)


def join_body(*refs):
    for i, ref in enumerate(refs[:-1]):
        refs[-1][i] = ref[0]


def shifted(ref, i, shift, gain_ref, at, y, put):
    rows, width = ref.shape[1:]
    off = ref[i].astype(F32) - shift
    gain = gain_ref[:, pl.ds(at, width)]
    y[:rows, put] = (off * gain).astype(BF16)
    y[rows:, put] = jnp.broadcast_to(gain, (y.shape[0] - rows, width)).astype(BF16)
    return off


def wide(column):
    return jnp.broadcast_to(column, (column.shape[0], 128))


def near_body(own_ref, prt_ref, gain_ref, g_ref, u_ref, *rest):
    ag_ref, au_ref, stat_ref, y = rest[-4:]
    me = lax.axis_index("tensor")
    core = lax.rem(me, 2)
    blocks, rows, width = own_ref.shape
    total = jnp.zeros((rows, width), F32)
    for i in range(blocks):
        total += own_ref[i].astype(F32) + prt_ref[i].astype(F32)
    shift = jnp.sum(total, axis=-1, keepdims=True) / (2 * blocks * width)
    square = jnp.zeros((rows, width), F32)
    for i in range(blocks):
        for ref, c in ((own_ref, core), (prt_ref, 1 - core)):
            at = pl.multiple_of(((me ^ (4 * i)) - core + c) * width, 128)
            put = pl.ds(pl.multiple_of((2 * i + c) * width, 128), width)
            off = shifted(ref, i, shift, gain_ref, at, y, put)
            square += off * off
    stat_ref[0] = wide(shift)
    stat_ref[1] = jnp.zeros_like(stat_ref[1])
    stat_ref[2] = wide(jnp.sum(square, axis=-1, keepdims=True))
    step = g_ref.shape[1] // 2
    for w_ref, out_ref in ((g_ref, ag_ref), (u_ref, au_ref)):
        for j in range(0, g_ref.shape[1], step):
            part = jnp.zeros((y.shape[0], step), F32)
            for i in range(blocks):
                at = pl.multiple_of(((me ^ (4 * i)) - core) * width, 128)
                part += dot(
                    y[:, 2 * i * width : 2 * (i + 1) * width], w_ref[pl.ds(at, 2 * width), j : j + step]
                )
            out_ref[:, j : j + step] = part


def far_body(flip, last, got_ref, gain_ref, g_ref, u_ref, ag_ref, au_ref, stat_ref, *rest):
    me = lax.axis_index("tensor") ^ flip
    rest = rest[-2 if last else -4 :]
    y = rest[-1]
    blocks, rows, width = got_ref.shape
    shift = stat_ref[0][:, :1]
    total = jnp.zeros((rows, width), F32)
    square = jnp.zeros((rows, width), F32)
    for i in range(blocks):
        at = pl.multiple_of((me ^ (4 * i)) * width, 128)
        off = shifted(got_ref, i, shift, gain_ref, at, y, slice(i * width, (i + 1) * width))
        total += off
        square += off * off
    first = stat_ref[1] + wide(jnp.sum(total, axis=-1, keepdims=True))
    second = stat_ref[2] + wide(jnp.sum(square, axis=-1, keepdims=True))
    if last:
        count = 4 * blocks * width
        lean = first[:, :1] / count
        scale = lax.rsqrt(jnp.maximum(second[:, :1] / count - lean * lean, 0.0) + 1e-05)
    else:
        rest[2][0], rest[2][1], rest[2][2] = stat_ref[0], first, second
    step = 256
    for j in range(0, g_ref.shape[1], step):
        cols = slice(j, j + step)
        parts = []
        for w_ref, acc_ref in ((g_ref, ag_ref), (u_ref, au_ref)):
            part = acc_ref[:, cols]
            for i in range(blocks):
                at = pl.multiple_of((me ^ (4 * i)) * width, 128)
                part += dot(y[:, i * width : (i + 1) * width], w_ref[pl.ds(at, width), cols])
            parts.append(part)
        if last:
            gated, lifted = [scale * (part[:rows] - lean * part[rows : rows + 1]) for part in parts]
            rest[0][:, cols] = (jax.nn.silu(gated) * lifted).astype(BF16)
        else:
            rest[0][:, cols], rest[1][:, cols] = parts


def down_body(other, h_ref, d_ref, out_ref):
    core = lax.rem(lax.axis_index("tensor") + other, 2)
    chips, rows, width = out_ref.shape
    for e in range(chips):
        at = pl.multiple_of((2 * e + core) * width, 128)
        out_ref[e] = dot(h_ref[...], d_ref[:, pl.ds(at, width)]).astype(BF16)


def add_body(a_ref, b_ref, out_ref):
    out_ref[...] = (a_ref[...].astype(F32) + b_ref[...].astype(F32)).astype(BF16)


def settle_body(got_ref, resid_ref, send_ref, after_ref):
    after = resid_ref[...] + jnp.sum(got_ref[...].astype(F32), axis=0)
    after_ref[...] = after
    for e in range(send_ref.shape[0]):
        send_ref[e] = after.astype(BF16)


def last_body(h_ref, d_ref, resid_ref, keep_ref, send_ref):
    me = lax.axis_index("tensor")
    core = lax.rem(me, 2)
    chips, rm, _ = keep_ref.shape
    rows, width = resid_ref.shape
    half = rows // 2
    to = lax.broadcasted_iota(jnp.int32, (rows, rows), 0)
    at = lax.broadcasted_iota(jnp.int32, (rows, rows), 1)
    rest = to % half
    side = jnp.where(to < half, core, 1 - core)
    moved = at == (2 * (rest // rm) + side) * rm + rest % rm
    hidden = dot(moved.astype(BF16), h_ref[...]).astype(BF16)
    resid = jnp.dot(
        moved.astype(F32), resid_ref[...], precision=lax.Precision.HIGHEST, preferred_element_type=F32
    )
    for k in range(d_ref.shape[1] // width):
        cols = slice(k * width, (k + 1) * width)
        part = dot(hidden, d_ref[:, cols]) + jnp.where(me == k, resid, 0.0)
        for e in range(chips):
            keep_ref[e, :, cols] = part[e * rm : (e + 1) * rm].astype(BF16)
            send_ref[e, :, cols] = part[half + e * rm : half + (e + 1) * rm].astype(BF16)


def final_body(got_ref, out_ref):
    out_ref[...] = jnp.sum(got_ref[...].astype(F32), axis=0).astype(BF16)


HELD = (('near', 'beside', 'across'), ('near', 'beside', 'across'))


FLOPS = {'project': 50000000000.0, 'attend': 20000000000.0, 'out': 3000000000.0, 'join': 1000000000.0, 'near': 1000000000.0, 'far': 500000000.0, 'down': 1000000000.0, 'add': 50000000000.0, 'settle': 50000000000.0}


def fast_local(
    n,
    token_ids,
    lengths,
    embed_table,
    gain_attn,
    w_qkv,
    w_out,
    gain_first,
    gate_first,
    up_first,
    down_first,
    gain_second,
    gate_second,
    up_second,
    down_second,
):
    rows_here, micro = token_ids.shape
    rows = n * rows_here * micro
    vocab, width = embed_table.shape
    chips = n // 2
    part = width // n
    same_core = [[2 * e + c for e in range(chips)] for c in range(2)]

    def exchange(x):
        return lax.all_to_all(x, "tensor", 0, 0, tiled=True, axis_index_groups=same_core)

    def partner(x):
        return lax.ppermute(x, "tensor", [(i, i ^ 1) for i in range(n)])

    def shape(dims, dtype=BF16):
        return jax.ShapeDtypeStruct(dims, dtype)

    rm = rows_here * micro
    pieces, ahead = 12, 5
    far = [pltpu.with_memory_space_constraint(x, pltpu.HBM) for x in (token_ids, embed_table, gain_attn[None], w_qkv)]
    triple = shape((vocab, part))
    t0, t1, t2, cols, marks = call(
        functools.partial(project_body, pieces, ahead),
        [triple] * 4 + [shape((n, -(-rm // 8) * 8, -(-vocab // 128) * 128), F32)],
        far,
        [HB] * 4,
        FLOPS["project"],
        24,
        [
            pltpu.SMEM(token_ids.shape, jnp.int32),
            pltpu.VMEM(embed_table.shape, BF16),
            pltpu.VMEM((1, width), F32),
            pltpu.VMEM(w_qkv.shape, BF16),
            pltpu.VMEM((vocab, width), BF16),
            pltpu.SemaphoreType.DMA((3,)),
            pltpu.SemaphoreType.DMA((pieces,)),
        ],
    )
    turn = pow(3, -1, n)
    t0 = lax.ppermute(t0, "tensor", [(d, (d - turn) % n) for d in range(n)])
    t2 = lax.ppermute(t2, "tensor", [(d, (d + turn) % n) for d in range(n)])
    hot = lax.all_to_all(marks, "tensor", 0, 0, tiled=True)
    share = shape((chips, rows, part))
    attended, embedded = call(
        functools.partial(attend_body, n, micro, rm),
        (shape((1, rows, part)), shape((rows, part), F32)),
        (lengths, hot, t0, t1, t2, cols),
        [SM] + [VM] * 5,
        FLOPS["attend"],
        2,
    )
    def toward(x, flip):
        return lax.ppermute(x, "tensor", [(i, i ^ flip) for i in range(n)])

    def along(sent):
        blocks = n // 4
        return call(
            join_body,
            shape((blocks, rows, part)),
            (sent, *[toward(sent, 4 * i) for i in range(1, blocks)]),
            [VM] * blocks,
            FLOPS["join"],
            2,
        )

    own = along(attended)
    beside = toward(own, 2)
    w_near = in_vmem(w_out)
    flat = shape((rows, part), F32)
    total = call(
        functools.partial(out_near_body, n), flat, (own, toward(own, 1), w_near), [VM] * 3, FLOPS["out"], 2
    )
    beside, total = lax.optimization_barrier((beside, total))
    across = toward(beside, 1)
    total = call(functools.partial(out_mid_body, n), flat, (beside, w_near, total), [VM] * 3, FLOPS["out"], 2)
    after_send, resid = call(
        functools.partial(out_far_body, n),
        (shape((1, rows, part)), flat),
        (across, w_near, total, embedded),
        [VM] * 4,
        FLOPS["out"],
        2,
    )

    def hidden_of(sent, gain, gate, up, down, held):
        keep = [[down] * (name in held) for name in ("near", "beside", "across")]
        blocks, units = n // 4, gate.shape[1]
        gain, gate, up = gain[None], in_vmem(gate), in_vmem(up)
        own = along(sent)
        beside = toward(own, 2)
        accs = (shape((rows + 16, units), F32), shape((rows + 16, units), F32), shape((3, rows, 128), F32))
        part_sums = call(
            near_body,
            accs,
            (own, toward(own, 1), gain, gate, up, *keep[0]),
            [VM] * (5 + len(keep[0])),
            FLOPS["near"],
            2,
            [pltpu.VMEM((rows + 16, 2 * blocks * part), BF16)],
        )
        y = [pltpu.VMEM((rows + 16, blocks * part), BF16)]
        beside, *part_sums = lax.optimization_barrier((beside, *part_sums))
        across = toward(beside, 1)
        part_sums = call(
            functools.partial(far_body, 2, False),
            accs,
            (beside, gain, gate, up, *part_sums, *keep[1]),
            [VM] * (7 + len(keep[1])),
            FLOPS["far"],
            1,
            y,
        )
        return call(
            functools.partial(far_body, 3, True),
            shape((rows, units)),
            (across, gain, gate, up, *part_sums, *keep[2]),
            [VM] * (7 + len(keep[2])),
            FLOPS["far"],
            1,
            y,
        )

    near = in_vmem(down_first)
    hidden = hidden_of(after_send, gain_first, gate_first, up_first, near, HELD[0])
    send, keep = [
        call(functools.partial(down_body, other), share, (hidden, near), [VM] * 2, FLOPS["down"], 2)
        for other in (1, 0)
    ]
    summed = call(add_body, share, (keep, partner(send)), [VM] * 2, FLOPS["add"], 2)
    first_send, resid = call(
        settle_body, (shape((1, rows, part)), shape((rows, part), F32)), (exchange(summed), resid), [VM] * 2, FLOPS["settle"], 2
    )
    near = in_vmem(down_second)
    hidden = hidden_of(first_send, gain_second, gate_second, up_second, near, HELD[1])
    blocks = shape((chips, rm, width))
    keep, send = call(last_body, (blocks, blocks), (hidden, near, resid), [VM] * 3, 1e9, 2)
    summed = call(add_body, blocks, (keep, partner(send)), [VM] * 2, 1e9, 2)
    out = call(final_body, shape((rm, width)), (exchange(summed),), [VM], 1e9, 2)
    return out.reshape(rows_here, micro, width)


def pick(mesh):
    n = mesh.shape["tensor"]
    if n % 4 == 0 and H % n == 0 and math.gcd(n, 3) == 1:
        return functools.partial(fast_local, n)
    return local


def solution(mesh):
    return jax.shard_map(
        pick(mesh),
        mesh=mesh,
        in_specs=(
            P("tensor", "groups"),
            P("groups"),
            P(),
            P(),
            P(None, "tensor"),
            P(None, "tensor"),
            P(),
            P(None, "tensor"),
            P(None, "tensor"),
            P("tensor", None),
            P(),
            P(None, "tensor"),
            P(None, "tensor"),
            P("tensor", None),
        ),
        out_specs=P("tensor", "groups", None),
        check_vma=False,
    )
```

```python
import functools
import math

import jax
import jax.numpy as jnp
from jax import lax
from jax.experimental import pallas as pl
from jax.experimental.pallas import tpu as pltpu
from jax.sharding import PartitionSpec as P

H = 48
HD = 128
F32 = jnp.float32
BF16 = jnp.bfloat16
VM = pl.BlockSpec(memory_space=pltpu.VMEM)
SM = pl.BlockSpec(memory_space=pltpu.SMEM)
HB = pl.BlockSpec(memory_space=pltpu.HBM)


def norm_rows(values, gain_vec):
    row_mean = jnp.mean(values, axis=-1, keepdims=True)
    centred = values - row_mean
    row_var = jnp.mean(centred * centred, axis=-1, keepdims=True)
    return (centred * lax.rsqrt(row_var + 1e-05) * gain_vec).astype(jnp.bfloat16)


def local_hidden(normed, gate_mat, up_mat):
    gated = jnp.einsum("pmd,dc->pmc", normed, gate_mat, preferred_element_type=jnp.float32)
    lifted = jnp.einsum("pmd,dc->pmc", normed, up_mat, preferred_element_type=jnp.float32)
    return (jax.nn.silu(gated) * lifted).astype(jnp.bfloat16)


def spread_rows(local_rows, row_fn):
    return row_fn(lax.all_gather(local_rows, "tensor", axis=0, tiled=True), jnp.int32(0))


def to_tokens(columns):
    return lax.all_to_all(columns, "tensor", split_axis=0, concat_axis=2, tiled=True)


def down_sum(hidden_all, down_mat):
    return lax.psum_scatter(
        jnp.einsum("pmc,cd->pmd", hidden_all, down_mat, preferred_element_type=jnp.float32),
        "tensor",
        scatter_dimension=0,
        tiled=True,
    )


def local(
    token_ids,
    lengths,
    embed_table,
    gain_attn,
    w_qkv,
    w_out,
    gain_first,
    gate_first,
    up_first,
    down_first,
    gain_second,
    gate_second,
    up_second,
    down_second,
):
    rows_here = token_ids.shape[0]
    micro_count = token_ids.shape[1]
    vocab_size = embed_table.shape[0]
    own_start = lax.axis_index("tensor") * rows_here
    onehot = (token_ids[:, :, None] == jnp.arange(vocab_size)[None, None, :]).astype(jnp.bfloat16)
    embedded = jnp.einsum("pmv,vd->pmd", onehot, embed_table, preferred_element_type=jnp.float32)
    normed_attn = norm_rows(embedded, gain_attn)

    def qkv_rows(row_piece, row_start):
        return jnp.einsum(
            "pmd,dc->pmc", row_piece, w_qkv, preferred_element_type=jnp.float32
        ).astype(jnp.bfloat16)

    projected = to_tokens(spread_rows(normed_attn, qkv_rows))
    feat_width = projected.shape[2] // 3
    queries = projected[..., :feat_width].reshape(rows_here, micro_count, H, HD)
    key_rows = projected[..., feat_width : 2 * feat_width]
    value_rows = projected[..., 2 * feat_width :]
    score_scale = HD ** (-0.5)
    key_piece = lax.all_gather(key_rows, "tensor", axis=0, tiled=True)
    value_piece = lax.all_gather(value_rows, "tensor", axis=0, tiled=True)
    piece_rows = key_piece.shape[0]
    key_heads = key_piece.reshape(piece_rows, micro_count, H, HD)
    value_heads = value_piece.reshape(piece_rows, micro_count, H, HD)
    scores = (
        jnp.einsum("pmhe,qmhe->pmhq", queries, key_heads, preferred_element_type=jnp.float32)
        * score_scale
    )
    positions = jnp.arange(piece_rows)
    live_keys = (positions[None, :] < lengths[:, None]).astype(jnp.float32)
    weights = jnp.exp(scores) * live_keys[None, :, None, :]
    denominator = jnp.sum(weights, axis=-1)
    numerator = jnp.einsum(
        "pmhq,qmhe->pmhe",
        weights.astype(jnp.bfloat16),
        value_heads,
        preferred_element_type=jnp.float32,
    )
    numerator, denominator = (numerator, denominator)
    attended = (
        (numerator / denominator[..., None])
        .reshape(rows_here, micro_count, feat_width)
        .astype(jnp.bfloat16)
    )

    def out_rows(row_piece, row_start):
        return jnp.einsum(
            "pmd,dc->pmc", row_piece, w_out, preferred_element_type=jnp.float32
        ).astype(jnp.bfloat16)

    after_attn = embedded + to_tokens(spread_rows(attended, out_rows)).astype(jnp.float32)

    def first_rows(row_piece, row_start):
        return local_hidden(row_piece, gate_first, up_first)

    hidden_first = spread_rows(norm_rows(after_attn, gain_first), first_rows)
    partial_all = jnp.einsum(
        "pmc,cd->pmd", hidden_first, down_first, preferred_element_type=jnp.float32
    )
    own_rows = lax.dynamic_slice_in_dim(partial_all, own_start, rows_here, 0) + after_attn
    partial_all = lax.dynamic_update_slice_in_dim(partial_all, own_rows, own_start, 0)
    first_all = lax.psum(partial_all, "tensor")
    after_first = lax.dynamic_slice_in_dim(first_all, own_start, rows_here, 0)
    hidden_second = local_hidden(norm_rows(first_all, gain_second), gate_second, up_second)
    after_second = after_first + down_sum(hidden_second, down_second)
    return after_second.astype(jnp.bfloat16)


def dot(a, b):
    return jnp.dot(a, b, preferred_element_type=F32)


def in_vmem(x):
    return pltpu.with_memory_space_constraint(x, pltpu.VMEM)


def call(body, out_shape, args, specs, flops, limit_mib, scratch=()):
    many = isinstance(out_shape, (tuple, list))
    return pl.pallas_call(
        body,
        out_shape=out_shape,
        in_specs=specs,
        out_specs=[VM] * len(out_shape) if many else VM,
        scratch_shapes=list(scratch),
        compiler_params=pltpu.CompilerParams(vmem_limit_bytes=limit_mib << 20),
        cost_estimate=pl.CostEstimate(flops=int(flops), transcendentals=0, bytes_accessed=1 << 20),
    )(*args)


def project_body(
    pieces, ahead, ids_hbm, table_hbm, gain_hbm, w_hbm, t0_ref, t1_ref, t2_ref, cols_ref, hot_ref,
    ids_ref, table, gain, w_buf, normed, sems, w_sems,
):
    me = lax.axis_index("tensor")
    depth = w_hbm.shape[0] // pieces
    small = [
        pltpu.make_async_copy(table_hbm, table, sems.at[0]),
        pltpu.make_async_copy(gain_hbm, gain, sems.at[1]),
    ]
    ids = pltpu.make_async_copy(ids_hbm, ids_ref, sems.at[2])
    ids.start()
    copies = [
        pltpu.make_async_copy(
            w_hbm.at[pl.ds(i * depth, depth)], w_buf.at[pl.ds(i * depth, depth)], w_sems.at[i]
        )
        for i in range(pieces)
    ]
    for one in small + copies[:2]:
        one.start()
    ids.wait()
    chips, height, lanes = hot_ref.shape
    rows_here, micro = ids_ref.shape
    row_at = lax.broadcasted_iota(jnp.int32, (height, lanes), 0)
    word_at = lax.broadcasted_iota(jnp.int32, (height, lanes), 1)
    hot = jnp.zeros((height, lanes), F32)
    for p in range(rows_here):
        for m in range(micro):
            here = (row_at == p * micro + m) & (word_at == ids_ref[p, m])
            hot = jnp.where(here, 1.0, hot)
    for i in range(chips):
        hot_ref[i] = hot
    for one in small:
        one.wait()
    for one in copies[2:ahead]:
        one.start()
    values = table[...].astype(F32)
    centred = values - jnp.mean(values, axis=-1, keepdims=True)
    var = jnp.mean(centred * centred, axis=-1, keepdims=True)
    normed[...] = (centred * lax.rsqrt(var + 1e-05) * gain[...]).astype(BF16)
    width = cols_ref.shape[1]
    cols_ref[...] = table[:, pl.ds(pl.multiple_of(me * width, 128), width)]
    total = jnp.zeros((normed.shape[0], w_hbm.shape[1]), F32)
    for i, one in enumerate(copies):
        one.wait()
        if i + ahead < pieces:
            copies[i + ahead].start()
        total += dot(normed[:, i * depth : (i + 1) * depth], w_buf[i * depth : (i + 1) * depth, :])
    for i, ref in enumerate((t0_ref, t1_ref, t2_ref)):
        ref[...] = total[:, i * width : (i + 1) * width].astype(BF16)


def owned(n, d):
    return lax.rem(3 * d + 1, n)


def attend_body(n, micro, rm, lens_ref, hot_ref, t0_ref, t1_ref, t2_ref, cols_ref, out_ref, emb_ref):
    head = owned(n, lax.axis_index("tensor"))
    vocab = cols_ref.shape[0]
    onehot = jnp.concatenate([hot_ref[p, :rm, :vocab] for p in range(hot_ref.shape[0])], axis=0).astype(BF16)
    emb_ref[...] = dot(onehot, cols_ref[...])
    got = [dot(onehot, ref[...]).astype(BF16) for ref in (t0_ref, t1_ref, t2_ref)]

    def block(b):
        at = lax.rem(head + b * n, 3)
        return jnp.where(at == 0, got[0], jnp.where(at == 1, got[1], got[2]))

    queries, keys, values = block(0), block(1), block(2)
    rows, width = queries.shape
    row_at = lax.broadcasted_iota(jnp.int32, (rows, rows), 0)
    key_at = lax.broadcasted_iota(jnp.int32, (rows, rows), 1)
    live = jnp.zeros((rows, rows), jnp.bool_)
    for m in range(micro):
        both = (row_at % micro == m) & (key_at % micro == m)
        live = live | (both & (key_at // micro < lens_ref[m]))
    for h in range(width // HD):
        cols = slice(h * HD, (h + 1) * HD)
        scores = lax.dot_general(
            queries[:, cols], keys[:, cols], (((1,), (1,)), ((), ())), preferred_element_type=F32
        ) * (HD ** (-0.5))
        weights = jnp.where(live, jnp.exp(scores), 0.0)
        denominator = jnp.sum(weights, axis=-1, keepdims=True)
        numerator = dot(weights.astype(BF16), values[:, cols])
        attended = (numerator / denominator).astype(BF16)
        for e in range(out_ref.shape[0]):
            out_ref[e, :, cols] = attended


def out_sum(n, flip, ref, w_ref):
    me = lax.axis_index("tensor") ^ flip
    blocks, rows, width = ref.shape
    total = jnp.zeros((rows, width), F32)
    for i in range(blocks):
        at = pl.multiple_of(owned(n, me ^ (4 * i)) * width, 128)
        total += dot(ref[i], w_ref[pl.ds(at, width), :])
    return total


def out_near_body(n, own_ref, prt_ref, w_ref, total_ref):
    total_ref[...] = out_sum(n, 0, own_ref, w_ref) + out_sum(n, 1, prt_ref, w_ref)


def out_mid_body(n, got_ref, w_ref, near_ref, total_ref):
    total_ref[...] = near_ref[...] + out_sum(n, 2, got_ref, w_ref)


def out_far_body(n, got_ref, w_ref, near_ref, emb_ref, send_ref, resid_ref):
    total = near_ref[...] + out_sum(n, 3, got_ref, w_ref)
    after = emb_ref[...] + total.astype(BF16).astype(F32)
    resid_ref[...] = after
    send_ref[0] = after.astype(BF16)


def join_body(*refs):
    for i, ref in enumerate(refs[:-1]):
        refs[-1][i] = ref[0]


def shifted(ref, i, shift, gain_ref, at, y, put):
    rows, width = ref.shape[1:]
    off = ref[i].astype(F32) - shift
    gain = gain_ref[:, pl.ds(at, width)]
    y[:rows, put] = (off * gain).astype(BF16)
    y[rows:, put] = jnp.broadcast_to(gain, (y.shape[0] - rows, width)).astype(BF16)
    return off


def wide(column):
    return jnp.broadcast_to(column, (column.shape[0], 128))


def near_body(own_ref, prt_ref, gain_ref, g_ref, u_ref, *rest):
    ag_ref, au_ref, stat_ref, y = rest[-4:]
    me = lax.axis_index("tensor")
    core = lax.rem(me, 2)
    blocks, rows, width = own_ref.shape
    total = jnp.zeros((rows, width), F32)
    for i in range(blocks):
        total += own_ref[i].astype(F32) + prt_ref[i].astype(F32)
    shift = jnp.sum(total, axis=-1, keepdims=True) / (2 * blocks * width)
    square = jnp.zeros((rows, width), F32)
    for i in range(blocks):
        for ref, c in ((own_ref, core), (prt_ref, 1 - core)):
            at = pl.multiple_of(((me ^ (4 * i)) - core + c) * width, 128)
            put = pl.ds(pl.multiple_of((2 * i + c) * width, 128), width)
            off = shifted(ref, i, shift, gain_ref, at, y, put)
            square += off * off
    stat_ref[0] = wide(shift)
    stat_ref[1] = jnp.zeros_like(stat_ref[1])
    stat_ref[2] = wide(jnp.sum(square, axis=-1, keepdims=True))
    step = g_ref.shape[1] // 2
    for w_ref, out_ref in ((g_ref, ag_ref), (u_ref, au_ref)):
        for j in range(0, g_ref.shape[1], step):
            part = jnp.zeros((y.shape[0], step), F32)
            for i in range(blocks):
                at = pl.multiple_of(((me ^ (4 * i)) - core) * width, 128)
                part += dot(
                    y[:, 2 * i * width : 2 * (i + 1) * width], w_ref[pl.ds(at, 2 * width), j : j + step]
                )
            out_ref[:, j : j + step] = part


def far_body(flip, last, got_ref, gain_ref, g_ref, u_ref, ag_ref, au_ref, stat_ref, *rest):
    me = lax.axis_index("tensor") ^ flip
    rest = rest[-2 if last else -4 :]
    y = rest[-1]
    blocks, rows, width = got_ref.shape
    shift = stat_ref[0][:, :1]
    total = jnp.zeros((rows, width), F32)
    square = jnp.zeros((rows, width), F32)
    for i in range(blocks):
        at = pl.multiple_of((me ^ (4 * i)) * width, 128)
        off = shifted(got_ref, i, shift, gain_ref, at, y, slice(i * width, (i + 1) * width))
        total += off
        square += off * off
    first = stat_ref[1] + wide(jnp.sum(total, axis=-1, keepdims=True))
    second = stat_ref[2] + wide(jnp.sum(square, axis=-1, keepdims=True))
    if last:
        count = 4 * blocks * width
        lean = first[:, :1] / count
        scale = lax.rsqrt(jnp.maximum(second[:, :1] / count - lean * lean, 0.0) + 1e-05)
    else:
        rest[2][0], rest[2][1], rest[2][2] = stat_ref[0], first, second
    step = g_ref.shape[1] // 2
    for j in range(0, g_ref.shape[1], step):
        cols = slice(j, j + step)
        parts = []
        for w_ref, acc_ref in ((g_ref, ag_ref), (u_ref, au_ref)):
            part = acc_ref[:, cols]
            for i in range(blocks):
                at = pl.multiple_of((me ^ (4 * i)) * width, 128)
                part += dot(y[:, i * width : (i + 1) * width], w_ref[pl.ds(at, width), cols])
            parts.append(part)
        if last:
            gated, lifted = [scale * (part[:rows] - lean * part[rows : rows + 1]) for part in parts]
            rest[0][:, cols] = (jax.nn.silu(gated) * lifted).astype(BF16)
        else:
            rest[0][:, cols], rest[1][:, cols] = parts


def down_body(other, h_ref, d_ref, out_ref):
    core = lax.rem(lax.axis_index("tensor") + other, 2)
    chips, rows, width = out_ref.shape
    for e in range(chips):
        at = pl.multiple_of((2 * e + core) * width, 128)
        out_ref[e] = dot(h_ref[...], d_ref[:, pl.ds(at, width)]).astype(BF16)


def add_body(a_ref, b_ref, out_ref):
    out_ref[...] = (a_ref[...].astype(F32) + b_ref[...].astype(F32)).astype(BF16)


def settle_body(got_ref, resid_ref, send_ref, after_ref):
    after = resid_ref[...] + jnp.sum(got_ref[...].astype(F32), axis=0)
    after_ref[...] = after
    for e in range(send_ref.shape[0]):
        send_ref[e] = after.astype(BF16)


def last_body(h_ref, d_ref, resid_ref, keep_ref, send_ref):
    me = lax.axis_index("tensor")
    core = lax.rem(me, 2)
    chips, rm, _ = keep_ref.shape
    rows, width = resid_ref.shape
    half = rows // 2
    to = lax.broadcasted_iota(jnp.int32, (rows, rows), 0)
    at = lax.broadcasted_iota(jnp.int32, (rows, rows), 1)
    rest = to % half
    side = jnp.where(to < half, core, 1 - core)
    moved = at == (2 * (rest // rm) + side) * rm + rest % rm
    hidden = dot(moved.astype(BF16), h_ref[...]).astype(BF16)
    resid = jnp.dot(
        moved.astype(F32), resid_ref[...], precision=lax.Precision.HIGHEST, preferred_element_type=F32
    )
    for k in range(d_ref.shape[1] // width):
        cols = slice(k * width, (k + 1) * width)
        part = dot(hidden, d_ref[:, cols]) + jnp.where(me == k, resid, 0.0)
        for e in range(chips):
            keep_ref[e, :, cols] = part[e * rm : (e + 1) * rm].astype(BF16)
            send_ref[e, :, cols] = part[half + e * rm : half + (e + 1) * rm].astype(BF16)


def final_body(got_ref, out_ref):
    out_ref[...] = jnp.sum(got_ref[...].astype(F32), axis=0).astype(BF16)


HELD = (('near', 'beside', 'across'), ('near', 'beside', 'across'))


FLOPS = {'project': 50000000000.0, 'attend': 20000000000.0, 'out': 3000000000.0, 'join': 1000000000.0, 'near': 1000000000.0, 'far': 500000000.0, 'down': 1000000000.0, 'add': 50000000000.0, 'settle': 50000000000.0}


def fast_local(
    n,
    token_ids,
    lengths,
    embed_table,
    gain_attn,
    w_qkv,
    w_out,
    gain_first,
    gate_first,
    up_first,
    down_first,
    gain_second,
    gate_second,
    up_second,
    down_second,
):
    rows_here, micro = token_ids.shape
    rows = n * rows_here * micro
    vocab, width = embed_table.shape
    chips = n // 2
    part = width // n
    same_core = [[2 * e + c for e in range(chips)] for c in range(2)]

    def exchange(x):
        return lax.all_to_all(x, "tensor", 0, 0, tiled=True, axis_index_groups=same_core)

    def partner(x):
        return lax.ppermute(x, "tensor", [(i, i ^ 1) for i in range(n)])

    def shape(dims, dtype=BF16):
        return jax.ShapeDtypeStruct(dims, dtype)

    rm = rows_here * micro
    pieces, ahead = 12, 5
    far = [pltpu.with_memory_space_constraint(x, pltpu.HBM) for x in (token_ids, embed_table, gain_attn[None], w_qkv)]
    triple = shape((vocab, part))
    t0, t1, t2, cols, marks = call(
        functools.partial(project_body, pieces, ahead),
        [triple] * 4 + [shape((n, -(-rm // 8) * 8, -(-vocab // 128) * 128), F32)],
        far,
        [HB] * 4,
        FLOPS["project"],
        24,
        [
            pltpu.SMEM(token_ids.shape, jnp.int32),
            pltpu.VMEM(embed_table.shape, BF16),
            pltpu.VMEM((1, width), F32),
            pltpu.VMEM(w_qkv.shape, BF16),
            pltpu.VMEM((vocab, width), BF16),
            pltpu.SemaphoreType.DMA((3,)),
            pltpu.SemaphoreType.DMA((pieces,)),
        ],
    )
    turn = pow(3, -1, n)
    t0 = lax.ppermute(t0, "tensor", [(d, (d - turn) % n) for d in range(n)])
    t2 = lax.ppermute(t2, "tensor", [(d, (d + turn) % n) for d in range(n)])
    hot = lax.all_to_all(marks, "tensor", 0, 0, tiled=True)
    share = shape((chips, rows, part))
    attended, embedded = call(
        functools.partial(attend_body, n, micro, rm),
        (shape((1, rows, part)), shape((rows, part), F32)),
        (lengths, hot, t0, t1, t2, cols),
        [SM] + [VM] * 5,
        FLOPS["attend"],
        2,
    )
    def toward(x, flip):
        return lax.ppermute(x, "tensor", [(i, i ^ flip) for i in range(n)])

    def along(sent):
        blocks = n // 4
        return call(
            join_body,
            shape((blocks, rows, part)),
            (sent, *[toward(sent, 4 * i) for i in range(1, blocks)]),
            [VM] * blocks,
            FLOPS["join"],
            2,
        )

    own = along(attended)
    beside = toward(own, 2)
    w_near = in_vmem(w_out)
    flat = shape((rows, part), F32)
    total = call(
        functools.partial(out_near_body, n), flat, (own, toward(own, 1), w_near), [VM] * 3, FLOPS["out"], 2
    )
    beside, total = lax.optimization_barrier((beside, total))
    across = toward(beside, 1)
    total = call(functools.partial(out_mid_body, n), flat, (beside, w_near, total), [VM] * 3, FLOPS["out"], 2)
    after_send, resid = call(
        functools.partial(out_far_body, n),
        (shape((1, rows, part)), flat),
        (across, w_near, total, embedded),
        [VM] * 4,
        FLOPS["out"],
        2,
    )

    def hidden_of(sent, gain, gate, up, down, held):
        keep = [[down] * (name in held) for name in ("near", "beside", "across")]
        blocks, units = n // 4, gate.shape[1]
        gain, gate, up = gain[None], in_vmem(gate), in_vmem(up)
        own = along(sent)
        beside = toward(own, 2)
        accs = (shape((rows + 16, units), F32), shape((rows + 16, units), F32), shape((3, rows, 128), F32))
        part_sums = call(
            near_body,
            accs,
            (own, toward(own, 1), gain, gate, up, *keep[0]),
            [VM] * (5 + len(keep[0])),
            FLOPS["near"],
            2,
            [pltpu.VMEM((rows + 16, 2 * blocks * part), BF16)],
        )
        y = [pltpu.VMEM((rows + 16, blocks * part), BF16)]
        beside, *part_sums = lax.optimization_barrier((beside, *part_sums))
        across = toward(beside, 1)
        part_sums = call(
            functools.partial(far_body, 2, False),
            accs,
            (beside, gain, gate, up, *part_sums, *keep[1]),
            [VM] * (7 + len(keep[1])),
            FLOPS["far"],
            1,
            y,
        )
        return call(
            functools.partial(far_body, 3, True),
            shape((rows, units)),
            (across, gain, gate, up, *part_sums, *keep[2]),
            [VM] * (7 + len(keep[2])),
            FLOPS["far"],
            1,
            y,
        )

    near = in_vmem(down_first)
    hidden = hidden_of(after_send, gain_first, gate_first, up_first, near, HELD[0])
    send, keep = [
        call(functools.partial(down_body, other), share, (hidden, near), [VM] * 2, FLOPS["down"], 2)
        for other in (1, 0)
    ]
    summed = call(add_body, share, (keep, partner(send)), [VM] * 2, FLOPS["add"], 2)
    first_send, resid = call(
        settle_body, (shape((1, rows, part)), shape((rows, part), F32)), (exchange(summed), resid), [VM] * 2, FLOPS["settle"], 2
    )
    near = in_vmem(down_second)
    hidden = hidden_of(first_send, gain_second, gate_second, up_second, near, HELD[1])
    blocks = shape((chips, rm, width))
    keep, send = call(last_body, (blocks, blocks), (hidden, near, resid), [VM] * 3, 1e9, 2)
    summed = call(add_body, blocks, (keep, partner(send)), [VM] * 2, 1e9, 2)
    out = call(final_body, shape((rm, width)), (exchange(summed),), [VM], 1e9, 2)
    return out.reshape(rows_here, micro, width)


def pick(mesh):
    n = mesh.shape["tensor"]
    if n % 4 == 0 and H % n == 0 and math.gcd(n, 3) == 1:
        return functools.partial(fast_local, n)
    return local


def solution(mesh):
    return jax.shard_map(
        pick(mesh),
        mesh=mesh,
        in_specs=(
            P("tensor", "groups"),
            P("groups"),
            P(),
            P(),
            P(None, "tensor"),
            P(None, "tensor"),
            P(),
            P(None, "tensor"),
            P(None, "tensor"),
            P("tensor", None),
            P(),
            P(None, "tensor"),
            P(None, "tensor"),
            P("tensor", None),
        ),
        out_specs=P("tensor", "groups", None),
        check_vma=False,
    )
```
